32 devices in a mesh: dp: 8 (over y, x, core), tensor: 4 (over z).
Axes of the slice: x: 2, y: 2, z: 4, core: 2. Of those that a mesh axis runs over, the one named last changes fastest.
Arguments:
- tokens: bfloat16 [8192, 2048], P('dp', 'tensor'), may hold values from -6 to 6
- cotangent: bfloat16 [8192, 2048], P('dp', 'tensor'), may hold values from -6 to 6
- first_gain: bfloat16 [2048], P('dp'), may hold values from 0.099609375 to 1.8984375
- first_shift: bfloat16 [2048], P('dp'), may hold values from -1.75 to 1.75
- attention_in: bfloat16 [3, 2048, 2048], P(None, 'dp', 'tensor'), may hold values from -0.125 to 0.125
- attention_bias: bfloat16 [2, 32, 64], P(None, 'tensor', 'dp'), may hold values from -3 to 3
- attention_out: bfloat16 [2048, 2048], P('tensor', 'dp'), may hold values from -0.5 to 0.5
- out_bias: bfloat16 [2048], P('dp'), may hold values from -1.75 to 1.75
- second_gain: bfloat16 [2048], P('dp'), may hold values from 0.099609375 to 1.8984375
- second_shift: bfloat16 [2048], P('dp'), may hold values from -1.75 to 1.75
- up_weight: bfloat16 [2048, 8192], P('dp', 'tensor'), may hold values from -0.125 to 0.125
- up_bias: bfloat16 [32, 256], P('tensor', 'dp'), may hold values from -3 to 3
- down_weight: bfloat16 [8192, 2048], P('tensor', 'dp'), may hold values from -0.0625 to 0.0625
- down_bias: bfloat16 [2048], P('dp'), may hold values from -1.75 to 1.75
- source_block: int32 [64], P('dp'), may hold values from 0 to 63, as said below
- target_block: int32 [64], P('dp'), may hold values from 0 to 63, as said below
- block_fill: int32 [64], P('dp'), may hold values from 1 to 128, as said below
- block_start: int32 [64], P('dp'), may hold values from 0 to 0, as said below
Outputs:
- output: bfloat16 [8192, 2048], P('dp', 'tensor')
- input_grad: bfloat16 [8192, 2048], P('dp', 'tensor')
- first_gain_grad: float32 [2048], P('dp')
- first_shift_grad: float32 [2048], P('dp')
- attention_in_grad: float32 [3, 2048, 2048], P(None, 'dp', 'tensor')
- attention_bias_grad: float32 [2, 32, 64], P(None, 'tensor', 'dp')
- attention_out_grad: float32 [2048, 2048], P('tensor', 'dp')
- out_bias_grad: float32 [2048], P('dp')
- second_gain_grad: float32 [2048], P('dp')
- second_shift_grad: float32 [2048], P('dp')
- up_weight_grad: float32 [2048, 8192], P('dp', 'tensor')
- up_bias_grad: float32 [32, 256], P('tensor', 'dp')
- down_weight_grad: float32 [8192, 2048], P('tensor', 'dp')
- down_bias_grad: float32 [2048], P('dp')
The draws below stay inside these ranges and needn't reach their ends.
Inputs may be any that keep to these rules, and one draw needn't show every extreme that they name: `source_block`: a permutation of the 64 anchor blocks. `target_block`: the inverse permutation of source_block. `block_fill`: 128 in every block but the last of a sequence; a sequence has 128 to 1024 tokens; the first sequence of every bin has 1024 tokens. `block_start`: every bin holds whole sequences of consecutive blocks, each of 1 to 8 blocks; blocks of one sequence share this value and the sequence's first block equals it; where a bin has more than 8 blocks, its last block is a sequence of its own.
All inputs are finite; a program needn't handle non-finite values.
Results may differ from the reference program's by a relative error of at most 0.024.
Values may be sent and summed in bfloat16 or wider, within the bound.
No kernel may reach another device: no remote copies, remote signals or barrier semaphores. Data moves between devices by JAX's collectives and lax.ppermute only.
A program may use at most 256 MiB of HBM per device.

```python
import jax
import jax.numpy as jnp
from jax import lax

D = 2048
H = 32
HD = 64
FF = 8192
BLK = 128
MAXLEN = 1024
QB = 512
BIN = 1024
TOKENS = 8192
NBLK = 64
BIN_BLK = 8
N_DP = 8
N_TENSOR = 4


def layout(key):
    mixed = jax.random.fold_in(key, 11)
    coin_key, fill_key, order_key = jax.random.split(mixed, 3)
    blocks_most = MAXLEN // BLK
    index = jnp.arange(NBLK, dtype=jnp.int32)
    inner = index % BIN_BLK
    coins = jax.random.randint(coin_key, (NBLK,), 0, 10)

    def walk(length, item):
        where_now, coin = item
        closing_slot = (where_now == BIN_BLK - 1) & (where_now >= blocks_most)
        fresh = (where_now == 0) | (where_now == blocks_most) | closing_slot | (where_now > blocks_most) & ((coin < 3) | (length >= blocks_most))
        length = jnp.where(fresh, 1, length + 1).astype(jnp.int32)
        return (length, fresh)
    ended, fresh = lax.scan(walk, jnp.int32(0), (inner, coins))
    head = lax.cummax(jnp.where(fresh, index, 0), axis=0)
    start = (head - (index - inner)).astype(jnp.int32)
    closing = jnp.concatenate([fresh[1:], jnp.ones((1,), dtype=bool)])
    partial_fill = jax.random.randint(fill_key, (NBLK,), 1, BLK + 1)
    fill = jnp.where(closing & jnp.logical_not(fresh) & (start != 0), partial_fill, BLK).astype(jnp.int32)
    labels = jax.random.permutation(order_key, NBLK).astype(jnp.int32)
    score = labels[head] * NBLK + index
    order = jnp.argsort(score).astype(jnp.int32)
    inverse = jnp.argsort(order).astype(jnp.int32)
    return (inverse, order, fill, start)


def draw_source_block(key, part):
    return layout(key)[0]


def draw_target_block(key, part):
    return layout(key)[1]


def draw_block_fill(key, part):
    return layout(key)[2]


def draw_block_start(key, part):
    return layout(key)[3]


def shard_levels(rng, extent, cuts, smallest, top_value):
    def one(axis_at, shards_of):
        draws = jax.random.uniform(jax.random.fold_in(jax.random.fold_in(rng, 6), axis_at), (shards_of,), jnp.float32, smallest / len(cuts), top_value / len(cuts))
        return jnp.repeat(jnp.exp(draws), extent[axis_at] // shards_of).reshape((-1,) + (1,) * (len(extent) - axis_at - 1))

    level = one(*cuts[0])
    for cut in cuts[1:]:
        level = level * one(*cut)
    return level


def gaussian(stream_key, dims, scale, most, cuts=(), kind=jnp.bfloat16):
    values = scale * jax.random.normal(stream_key, dims, jnp.float32)
    if cuts:
        values = values * shard_levels(stream_key, dims, cuts, -0.22, 0.18)
    return jnp.clip(values, -most, most).astype(kind)


def setup_inputs(seed: int = 0) -> dict:
    key_of = jax.random.split(jax.random.key(seed), 19)
    return {
        "tokens": gaussian(key_of[0], (TOKENS, D), 1.0, 6.0, ((0, 8), (1, 4))),
        "cotangent": gaussian(key_of[1], (TOKENS, D), 1.0, 6.0, ((0, 8), (1, 4))),
        "first_gain": jnp.clip(1.0 + 0.18 * jax.random.normal(key_of[2], (D,), jnp.float32), 0.099609375, 1.8984375).astype(jnp.bfloat16),
        "first_shift": gaussian(key_of[3], (D,), 0.3, 1.75, ((0, 8),)),
        "attention_in": gaussian(key_of[4], (3, D, D), D ** -0.5, 0.125, ((1, 8), (2, 4))),
        "attention_bias": gaussian(key_of[5], (2, H, HD), 0.5, 3.0, ((1, 4), (2, 8))),
        "attention_out": gaussian(key_of[6], (D, D), (D // 16) ** -0.5, 0.5, ((0, 4), (1, 8))),
        "out_bias": gaussian(key_of[7], (D,), 0.3, 1.75, ((0, 8),)),
        "second_gain": jnp.clip(1.0 + 0.18 * jax.random.normal(key_of[8], (D,), jnp.float32), 0.099609375, 1.8984375).astype(jnp.bfloat16),
        "second_shift": gaussian(key_of[9], (D,), 0.3, 1.75, ((0, 8),)),
        "up_weight": gaussian(key_of[10], (D, FF), D ** -0.5, 0.125, ((0, 8), (1, 4))),
        "up_bias": gaussian(key_of[11], (H, FF // H), 0.5, 3.0, ((0, 4), (1, 8))),
        "down_weight": gaussian(key_of[12], (FF, D), FF ** -0.5, 0.0625, ((0, 4), (1, 8))),
        "down_bias": gaussian(key_of[13], (D,), 0.3, 1.75, ((0, 8),)),
        "source_block": draw_source_block(jax.random.fold_in(key_of[18], 71), 0),
        "target_block": draw_target_block(jax.random.fold_in(key_of[18], 71), 0),
        "block_fill": draw_block_fill(jax.random.fold_in(key_of[18], 71), 0),
        "block_start": draw_block_start(jax.random.fold_in(key_of[18], 71), 0),
    }


@jax.custom_vjp
def low(v):
    return lax.optimization_barrier(v.astype(jnp.bfloat16)).astype(jnp.float32)

@jax.custom_vjp
def low_back(v):
    return v

def low_keep(v):
    return (low(v), None)

def low_pass(kept, grad):
    return (grad,)

def back_keep(v):
    return (v, None)

def back_low(kept, grad):
    return (low(grad),)
low.defvjp(low_keep, low_pass)
low_back.defvjp(back_keep, back_low)
masked_score = -1e+30

def product(left, right):
    return jnp.dot(left, right, precision=lax.Precision.HIGHEST)

def layer_norm(values, gain, shift):
    mean = lax.optimization_barrier(jnp.mean(values, axis=-1, keepdims=True))
    centred = values - mean
    variance = lax.optimization_barrier(jnp.mean(centred * centred, axis=-1, keepdims=True))
    return centred * lax.rsqrt(variance + 1e-05) * gain + shift

def grouped_sum(left, right):
    group = left.shape[1] // N_TENSOR
    total = jnp.zeros((left.shape[0], right.shape[1]), jnp.float32)
    for index in range(N_TENSOR):
        lo_col = index * group
        total = total + low(product(left[:, lo_col:lo_col + group], right[lo_col:lo_col + group]))
    return total

def grouped_in(inputs, weights):
    group = weights.shape[1] // N_TENSOR
    pieces = []
    for index in range(N_TENSOR):
        lo_col = index * group
        shared = low_back(inputs)
        pieces.append(product(shared, weights[:, lo_col:lo_col + group]))
    return jnp.concatenate(pieces, axis=1)

def grouped_three(inputs, first, second, third):
    group = first.shape[1] // N_TENSOR
    pieces_a, pieces_b, pieces_c = ([], [], [])
    for index in range(N_TENSOR):
        lo_col = index * group
        shared = low_back(inputs)
        pieces_a.append(product(shared, first[:, lo_col:lo_col + group]))
        pieces_b.append(product(shared, second[:, lo_col:lo_col + group]))
        pieces_c.append(product(shared, third[:, lo_col:lo_col + group]))
    return (jnp.concatenate(pieces_a, axis=1), jnp.concatenate(pieces_b, axis=1), jnp.concatenate(pieces_c, axis=1))

def attend(query, keys, values, segment, place, valid):
    slots = query.shape[0]
    width = query.shape[1]
    keys_pad = jnp.concatenate([jnp.zeros((MAXLEN, width), jnp.float32), keys])
    values_pad = jnp.concatenate([jnp.zeros((MAXLEN, width), jnp.float32), values])
    segment_pad = jnp.concatenate([jnp.full((MAXLEN,), -1, jnp.int32), segment])
    place_pad = jnp.concatenate([jnp.zeros((MAXLEN,), jnp.int32), place])
    valid_pad = jnp.concatenate([jnp.zeros((MAXLEN,), dtype=bool), valid])
    slopes = jnp.exp2(-8.0 * (jnp.arange(H, dtype=jnp.int32) + 1).astype(jnp.float32) / H)
    window = QB + MAXLEN

    def one_block(index):
        begin = (index * QB).astype(jnp.int32)
        query_block = lax.dynamic_slice_in_dim(query, begin, QB).reshape(QB, H, HD)
        key_block = lax.dynamic_slice_in_dim(keys_pad, begin, window).reshape(window, H, HD)
        value_block = lax.dynamic_slice_in_dim(values_pad, begin, window).reshape(window, H, HD)
        query_segment = lax.dynamic_slice_in_dim(segment, begin, QB)
        query_place = lax.dynamic_slice_in_dim(place, begin, QB)
        key_segment = lax.dynamic_slice_in_dim(segment_pad, begin, window)
        key_place = lax.dynamic_slice_in_dim(place_pad, begin, window)
        key_valid = lax.dynamic_slice_in_dim(valid_pad, begin, window)
        raw = jnp.einsum('qhe,khe->hqk', query_block, key_block, precision=lax.Precision.HIGHEST) * 0.125
        distance = (query_place[:, None] - key_place[None, :]).astype(jnp.float32)
        raw = raw - slopes[:, None, None] * distance[None]
        allowed = (query_segment[:, None] == key_segment[None, :]) & (key_place[None, :] <= query_place[:, None]) & key_valid[None, :]
        scores = low_back(jnp.where(allowed[None], raw, masked_score))
        weights = low(jax.nn.softmax(scores, axis=-1))
        mixed = jnp.einsum('hqk,khe->qhe', weights, value_block, precision=lax.Precision.HIGHEST)
        return mixed.reshape(QB, width)
    blocks = lax.map(jax.checkpoint(one_block), jnp.arange(slots // QB, dtype=jnp.int32))
    return blocks.reshape(slots, width)

def block_layer(params, rows, fill, start):
    gain_one, shift_one, in_proj, attn_bias, out_proj, out_shift, gain_two, shift_two, up_full, up_shift, down_full, down_shift = params
    slots = rows.shape[0]
    slot_index = jnp.arange(slots, dtype=jnp.int32)
    offset = slot_index % BLK
    block_of = slot_index // BLK
    segment = start[block_of]
    valid = offset < fill[block_of]
    place = (block_of - segment) * BLK + offset
    norm_one = low(layer_norm(rows, gain_one, shift_one))
    query_raw, keys_raw, values_raw = grouped_three(norm_one, in_proj[0], in_proj[1], in_proj[2])
    query = low(low_back(query_raw + attn_bias[0].reshape(-1)))
    keys = low(low_back(keys_raw))
    values = low(low_back(values_raw + attn_bias[1].reshape(-1)))
    attended = low(low_back(attend(query, keys, values, segment, place, valid)))
    resid = rows + low_back(grouped_sum(attended, out_proj)) + out_shift
    norm_two = low(layer_norm(resid, gain_two, shift_two))
    before = low_back(grouped_in(norm_two, up_full) + up_shift.reshape(-1))
    hidden = low(jax.nn.gelu(before, approximate=False))
    result = resid + low_back(grouped_sum(hidden, down_full)) + down_shift
    return jnp.where(valid[:, None], result, 0.0)

def reference(tokens, cotangent, first_gain, first_shift, attention_in, attention_bias, attention_out, out_bias, second_gain, second_shift, up_weight, up_bias, down_weight, down_bias, source_block, target_block, block_fill, block_start):
    params = tuple((item.astype(jnp.float32) for item in (first_gain, first_shift, attention_in, attention_bias, attention_out, out_bias, second_gain, second_shift, up_weight, up_bias, down_weight, down_bias)))

    def to_bins(array):
        return array.astype(jnp.float32).reshape(NBLK, BLK, D)[source_block].reshape(N_DP, BIN, D)
    rows_all = to_bins(tokens)
    grads_all = to_bins(cotangent)
    fills = block_fill.reshape(N_DP, BIN_BLK)
    starts = block_start.reshape(N_DP, BIN_BLK)

    def one_bin(total, items):
        rows, grad, fill, start = items
        result, pull = jax.vjp(lambda weights, inputs: block_layer(weights, inputs, fill, start), params, rows)
        weight_grads, input_grads = pull(grad)
        return (jax.tree.map(jnp.add, total, weight_grads), (result, input_grads))
    zeros = jax.tree.map(jnp.zeros_like, params)
    total, (results, input_grads) = lax.scan(one_bin, zeros, (rows_all, grads_all, fills, starts))

    def to_anchor(array):
        return array.reshape(NBLK, BLK, D)[target_block].reshape(TOKENS, D).astype(jnp.bfloat16)
    return (to_anchor(results), to_anchor(input_grads), total[0], total[1], total[2], total[3], total[4], total[5], total[6], total[7], total[8], total[9], total[10], total[11])
```

```python
import jax
import jax.numpy as jnp
from jax import lax
from jax.experimental import pallas as pl
from jax.experimental.pallas import tpu as pltpu
from jax.sharding import PartitionSpec as P

H = 32
BLK = 128
MAXLEN = 1024
QB = 512
TILE = 256

norm_eps = 1e-05
masked_score = -1e30
density_scale = 0.3989422804014327
root_half = 0.7071067811865476

f32 = jnp.float32
bf16 = jnp.bfloat16


def normalize(rows):
    mean = jnp.mean(rows, axis=-1, keepdims=True)
    centred = rows - mean
    variance = jnp.mean(centred * centred, axis=-1, keepdims=True)
    scale = lax.rsqrt(variance + norm_eps)
    return (centred * scale, scale)


def norm_back(grad_norm, unit, scale, gain):
    grad_unit = grad_norm * gain
    mean_grad = jnp.mean(grad_unit, axis=-1, keepdims=True)
    mean_dot = jnp.mean(grad_unit * unit, axis=-1, keepdims=True)
    return scale * (grad_unit - mean_grad - unit * mean_dot)


def spread(table):
    return jnp.broadcast_to(table[:, None], (table.shape[0], BLK)).reshape(-1)


def swap(value, k):
    count = lax.axis_size("dp")
    return lax.ppermute(value, "dp", [(i, i ^ k) for i in range(count)])


def turn(value, r):
    count = lax.axis_size("tensor")
    return lax.ppermute(value, "tensor", [(i, (i + r) % count) for i in range(count)])


def after(values, others):
    return lax.optimization_barrier((values, others))[0]


def near_kinds():
    count = lax.axis_size("dp")
    return [0, 2, 6, 4] if count == 8 else list(range(0, count, 2))


def plane_gather(rows):
    if lax.axis_size("dp") == 8:
        half = rows.shape[1] // 2
        a = swap(rows, 2)
        b = swap(rows, 4)
        corner = [swap(a[:, :half], 4), swap(b[:, half:], 2)]
        pieces = [rows, a, jnp.concatenate(corner, axis=1), b]
    else:
        pieces = [swap(rows, k) if k else rows for k in near_kinds()]
    near = jnp.concatenate(pieces, axis=0)
    return near, swap(near, 1)


def plane_sum(near, far, weight, dim):
    count = lax.axis_size("dp")
    step = near.shape[0] * 2 // count
    other = swap(contract(far, weight, 1, dim).astype(bf16), 1)
    both = (contract(near, weight, 1, dim) + other.astype(f32)).astype(bf16)
    if count == 8:
        half = both.shape[1] // 2
        a = swap(both[step : 3 * step, :half], 2)
        b = swap(both[2 * step :, half:], 4)
        c = both[3 * step :, :half].astype(f32) + a[step:].astype(f32)
        d = both[step : 2 * step, half:].astype(f32) + b[:step].astype(f32)
        c = swap(c.astype(bf16), 4)
        d = swap(d.astype(bf16), 2)
        left = both[:step, :half].astype(f32) + a[:step].astype(f32) + c.astype(f32)
        right = both[:step, half:].astype(f32) + b[step:].astype(f32) + d.astype(f32)
        return jnp.concatenate([left, right], axis=1)
    total = both[:step].astype(f32)
    for j, k in enumerate(near_kinds()):
        if k:
            total = total + swap(both[j * step : (j + 1) * step], k).astype(f32)
    return total


def small_gather(value):
    count = lax.axis_size("dp")
    value = value.reshape(1, -1)
    k = 1
    while k < count:
        value = jnp.concatenate([value, swap(value, k)], axis=0)
        k *= 2
    return jnp.take(value, jnp.arange(count, dtype=jnp.int32) ^ lax.axis_index("dp"), axis=0)


def pick_blocks(near, far, owner, local, blocks):
    rank = lax.axis_index("dp")
    near = near.reshape(-1, BLK, near.shape[-1])
    far = far.reshape(-1, BLK, far.shape[-1])
    kinds = near_kinds()
    piece = jnp.array([kinds.index(2 * j) for j in range(len(kinds))], jnp.int32)
    k = owner ^ rank
    at = piece[k // 2] * blocks + local
    picked = []
    for i in range(owner.shape[0]):
        a = lax.dynamic_index_in_dim(near, at[i], 0, keepdims=True)
        b = lax.dynamic_index_in_dim(far, at[i], 0, keepdims=True)
        picked.append(jnp.where(k[i] % 2 == 0, a, b))
    return jnp.concatenate(picked, axis=0)


def to_bins(blocks, here):
    count = lax.axis_size("tensor")
    z = lax.axis_index("tensor")
    wide = blocks.shape[-1]
    out = jnp.zeros((here, BLK, wide * count), blocks.dtype)
    for r in range(count):
        piece = lax.dynamic_slice_in_dim(blocks, ((z + r) % count) * here, here, 0)
        if r:
            piece = turn(piece, r)
        out = lax.dynamic_update_slice(out, piece, (0, 0, ((z - r) % count) * wide))
    return out


def from_bins(rows):
    count = lax.axis_size("tensor")
    z = lax.axis_index("tensor")
    here = rows.shape[0]
    wide = rows.shape[-1] // count
    out = jnp.zeros((here * count, BLK, wide), rows.dtype)
    for r in range(count):
        piece = lax.dynamic_slice_in_dim(rows, ((z + r) % count) * wide, wide, 2)
        if r:
            piece = turn(piece, r)
        out = lax.dynamic_update_slice(out, piece, (((z - r) % count) * here, 0, 0))
    return out


def contract(a, b, left, right):
    return lax.dot_general(a, b, (((left,), (right,)), ((), ())), preferred_element_type=f32)


def attend_kernel(heads, head_size, where, slopes, near, far, out_near, out_far, qkv, mixed):
    width = heads * head_size
    blocks = near.shape[0] // BLK
    for j in range(2 * blocks):
        source, i = (near, j) if j < blocks else (far, j - blocks)
        at = pl.multiple_of(where[j] * BLK, BLK)
        for part in range(3):
            for h in range(heads):
                lo = part * width + h * head_size
                piece = source[i * BLK : (i + 1) * BLK, lo : lo + head_size]
                if part == 0:
                    piece = (piece.astype(f32) * 0.125).astype(bf16)
                qkv[part, h, pl.ds(at, BLK), :] = piece
    slots = 2 * blocks * BLK

    def one_head(h, carry):
        slope = slopes[h]
        for t in range(slots // TILE):
            lo, hi = t * TILE, (t + 1) * TILE
            query = qkv[0, h, lo:hi, :]
            scores = contract(query, qkv[1, h, 0:hi, :], 1, 1)
            column = lax.broadcasted_iota(jnp.int32, (1, hi), 1)
            scores = scores + slope * (column - hi).astype(f32)
            diagonal = scores[:, lo:hi]
            rows = lax.broadcasted_iota(jnp.int32, (TILE, TILE), 0)
            columns = lax.broadcasted_iota(jnp.int32, (TILE, TILE), 1)
            diagonal = jnp.where(columns <= rows, diagonal, masked_score)
            scores = jnp.concatenate([scores[:, :lo], diagonal], axis=1) if t else diagonal
            top = jnp.max(scores, axis=1, keepdims=True)
            weights = jnp.exp(scores - top)
            total = jnp.sum(weights, axis=1, keepdims=True)
            result = contract(weights.astype(bf16), qkv[2, h, 0:hi, :], 1, 0) / total
            mixed[h, lo:hi, :] = result.astype(bf16)
        return carry

    lax.fori_loop(0, heads, one_head, 0)
    for j in range(2 * blocks):
        target, i = (out_near, j) if j < blocks else (out_far, j - blocks)
        at = pl.multiple_of(where[j] * BLK, BLK)
        for h in range(heads):
            target[i * BLK : (i + 1) * BLK, h * head_size : (h + 1) * head_size] = mixed[
                h, pl.ds(at, BLK), :
            ]


def attend_back_kernel(
    heads, head_size, where, slopes, near, far, grad_near, grad_far, out_near, out_far, qkvg, sums, parts
):
    width = heads * head_size
    blocks = near.shape[0] // BLK
    for j in range(2 * blocks):
        source, grad, i = (near, grad_near, j) if j < blocks else (far, grad_far, j - blocks)
        at = pl.multiple_of(where[j] * BLK, BLK)
        for part in range(4):
            for h in range(heads):
                lo = part * width + h * head_size
                if part < 3:
                    piece = source[i * BLK : (i + 1) * BLK, lo : lo + head_size]
                else:
                    piece = grad[i * BLK : (i + 1) * BLK, h * head_size : (h + 1) * head_size]
                if part == 0:
                    piece = (piece.astype(f32) * 0.125).astype(bf16)
                qkvg[part, h, pl.ds(at, BLK), :] = piece
    slots = 2 * blocks * BLK

    def one_head(h, carry):
        slope = slopes[h]
        sums[...] = jnp.zeros_like(sums)
        for t in range(slots // TILE):
            lo, hi = t * TILE, (t + 1) * TILE
            query = qkvg[0, h, lo:hi, :]
            grad = qkvg[3, h, lo:hi, :]
            keys = qkvg[1, h, 0:hi, :]
            scores = contract(keys, query, 1, 1)
            key_place = lax.broadcasted_iota(jnp.int32, (hi, 1), 0)
            scores = scores + slope * (key_place - hi).astype(f32)
            diagonal = scores[lo:hi, :]
            rows = lax.broadcasted_iota(jnp.int32, (TILE, TILE), 0)
            columns = lax.broadcasted_iota(jnp.int32, (TILE, TILE), 1)
            diagonal = jnp.where(rows <= columns, diagonal, masked_score)
            scores = jnp.concatenate([scores[:lo, :], diagonal], axis=0) if t else diagonal
            top = jnp.max(scores, axis=0, keepdims=True)
            weights = jnp.exp(scores - top)
            total = jnp.sum(weights, axis=0, keepdims=True)
            probs = weights * (1.0 / total)
            grad_probs = contract(qkvg[2, h, 0:hi, :], grad, 1, 1)
            inner = jnp.sum(probs * grad_probs, axis=0, keepdims=True)
            grad_scores = (probs * (grad_probs - inner)).astype(bf16)
            sums[0, 0:hi, :] += contract(grad_scores, query, 1, 0)
            sums[1, 0:hi, :] += contract(probs.astype(bf16), grad, 1, 0)
            grad_query = contract(grad_scores, keys, 0, 0) * 0.125
            parts[0, h, lo:hi, :] = grad_query.astype(bf16)
        parts[1, h] = sums[0].astype(bf16)
        parts[2, h] = sums[1].astype(bf16)
        return carry

    lax.fori_loop(0, heads, one_head, 0)
    for j in range(2 * blocks):
        target, i = (out_near, j) if j < blocks else (out_far, j - blocks)
        at = pl.multiple_of(where[j] * BLK, BLK)
        for part in range(3):
            for h in range(heads):
                lo = part * width + h * head_size
                target[i * BLK : (i + 1) * BLK, lo : lo + head_size] = parts[part, h, pl.ds(at, BLK), :]


def smem():
    return pl.BlockSpec(memory_space=pltpu.SMEM)


def vmem():
    return pl.BlockSpec(memory_space=pltpu.VMEM)


def attend_one(near, far, where, slopes, heads, head_size):
    slots = 2 * near.shape[0]
    width = heads * head_size
    half = jax.ShapeDtypeStruct((near.shape[0], width), bf16)

    def body(*refs):
        attend_kernel(heads, head_size, *refs)

    return pl.pallas_call(
        body,
        out_shape=(half, half),
        in_specs=[smem(), smem(), vmem(), vmem()],
        out_specs=(vmem(), vmem()),
        scratch_shapes=[
            pltpu.VMEM((3, heads, slots, head_size), bf16),
            pltpu.VMEM((heads, slots, head_size), bf16),
        ],
        cost_estimate=pl.CostEstimate(
            flops=2 * slots * slots * width, transcendentals=slots * slots * heads // 2, bytes_accessed=8 * slots * width
        ),
        name="attend",
    )(where, slopes, near, far)


def attend_one_back(near, far, grad_near, grad_far, where, slopes, heads, head_size):
    slots = 2 * near.shape[0]
    half = jax.ShapeDtypeStruct(near.shape, bf16)

    def body(*refs):
        attend_back_kernel(heads, head_size, *refs)

    return pl.pallas_call(
        body,
        out_shape=(half, half),
        in_specs=[smem(), smem(), vmem(), vmem(), vmem(), vmem()],
        out_specs=(vmem(), vmem()),
        scratch_shapes=[
            pltpu.VMEM((4, heads, slots, head_size), bf16),
            pltpu.VMEM((2, slots, head_size), f32),
            pltpu.VMEM((3, heads, slots, head_size), bf16),
        ],
        cost_estimate=pl.CostEstimate(
            flops=5 * slots * slots * heads * head_size,
            transcendentals=slots * slots * heads // 2,
            bytes_accessed=16 * slots * heads * head_size,
        ),
        name="attend_back",
    )(where, slopes, near, far, grad_near, grad_far)


def reorder(near, far, order):
    pieces = jnp.concatenate([near, far], axis=0).reshape(-1, BLK, near.shape[-1])
    return jnp.take(pieces, order, axis=0).reshape(-1, near.shape[-1])


def block_view(query, keys, values, segment, place, valid, slopes, heads, head_size):
    width = heads * head_size
    keys_pad = jnp.concatenate([jnp.zeros((MAXLEN, width), bf16), keys])
    values_pad = jnp.concatenate([jnp.zeros((MAXLEN, width), bf16), values])
    segment_pad = jnp.concatenate([jnp.full((MAXLEN,), -1, jnp.int32), segment])
    place_pad = jnp.concatenate([jnp.zeros((MAXLEN,), jnp.int32), place])
    valid_pad = jnp.concatenate([jnp.zeros((MAXLEN,), dtype=bool), valid])
    window = QB + MAXLEN

    def block_scores(begin):
        query_block = lax.dynamic_slice_in_dim(query, begin, QB).reshape(QB, heads, head_size)
        key_block = lax.dynamic_slice_in_dim(keys_pad, begin, window).reshape(window, heads, head_size)
        value_block = lax.dynamic_slice_in_dim(values_pad, begin, window).reshape(window, heads, head_size)
        query_segment = lax.dynamic_slice_in_dim(segment, begin, QB)
        query_place = lax.dynamic_slice_in_dim(place, begin, QB)
        key_segment = lax.dynamic_slice_in_dim(segment_pad, begin, window)
        key_place = lax.dynamic_slice_in_dim(place_pad, begin, window)
        key_valid = lax.dynamic_slice_in_dim(valid_pad, begin, window)
        raw = jnp.einsum("qhe,khe->hqk", query_block, key_block, preferred_element_type=f32) * 0.125
        distance = (query_place[:, None] - key_place[None, :]).astype(f32)
        raw = raw - slopes[:, None, None] * distance[None]
        allowed = (
            (query_segment[:, None] == key_segment[None, :])
            & (key_place[None, :] <= query_place[:, None])
            & key_valid[None, :]
        )
        return (jnp.where(allowed[None], raw, masked_score), query_block, key_block, value_block)

    return block_scores, window


def attend_any(query, keys, values, segment, place, valid, slopes, heads, head_size):
    slots, width = query.shape
    block_scores, _ = block_view(query, keys, values, segment, place, valid, slopes, heads, head_size)

    def forward_block(index, attended):
        begin = index * QB
        scores, _, _, value_block = block_scores(begin)
        weights = jax.nn.softmax(scores, axis=-1).astype(bf16)
        mixed = jnp.einsum("hqk,khe->qhe", weights, value_block, preferred_element_type=f32)
        return lax.dynamic_update_slice_in_dim(attended, mixed.reshape(QB, width).astype(bf16), begin, 0)

    return lax.fori_loop(0, slots // QB, forward_block, jnp.zeros((slots, width), bf16))


def attend_any_back(query, keys, values, grad, segment, place, valid, slopes, heads, head_size):
    slots, width = query.shape
    block_scores, window = block_view(query, keys, values, segment, place, valid, slopes, heads, head_size)

    def backward_block(index, carry):
        grad_query, grad_keys, grad_values = carry
        begin = index * QB
        scores, query_block, key_block, value_block = block_scores(begin)
        probs = jax.nn.softmax(scores, axis=-1)
        grad_block = lax.dynamic_slice_in_dim(grad, begin, QB).reshape(QB, heads, head_size)
        grad_probs = jnp.einsum("qhe,khe->hqk", grad_block, value_block, preferred_element_type=f32)
        inner = jnp.sum(probs * grad_probs, axis=-1, keepdims=True)
        grad_scores = (probs * (grad_probs - inner)).astype(bf16)
        query_part = jnp.einsum("hqk,khe->qhe", grad_scores, key_block, preferred_element_type=f32) * 0.125
        key_part = jnp.einsum("hqk,qhe->khe", grad_scores, query_block, preferred_element_type=f32) * 0.125
        value_part = jnp.einsum("hqk,qhe->khe", probs.astype(bf16), grad_block, preferred_element_type=f32)
        grad_query = lax.dynamic_update_slice_in_dim(grad_query, query_part.reshape(QB, width), begin, 0)
        old_keys = lax.dynamic_slice_in_dim(grad_keys, begin, window)
        grad_keys = lax.dynamic_update_slice_in_dim(
            grad_keys, old_keys + key_part.reshape(window, width), begin, 0
        )
        old_values = lax.dynamic_slice_in_dim(grad_values, begin, window)
        grad_values = lax.dynamic_update_slice_in_dim(
            grad_values, old_values + value_part.reshape(window, width), begin, 0
        )
        return (grad_query, grad_keys, grad_values)

    padded_zero = jnp.zeros((MAXLEN + slots, width), f32)
    grad_query, grad_keys, grad_values = lax.fori_loop(
        0, slots // QB, backward_block, (jnp.zeros((slots, width), f32), padded_zero, padded_zero)
    )
    return jnp.concatenate([grad_query, grad_keys[MAXLEN:], grad_values[MAXLEN:]], axis=1).astype(bf16)


def on_device(
    tokens,
    cotangent,
    first_gain,
    first_shift,
    attention_in,
    attention_bias,
    attention_out,
    out_bias,
    second_gain,
    second_shift,
    up_weight,
    up_bias,
    down_weight,
    down_bias,
    source_block,
    target_block,
    block_fill,
    block_start,
):
    n = lax.axis_size("dp")
    nz = lax.axis_size("tensor")
    p = lax.axis_index("dp")
    z = lax.axis_index("tensor")
    bin_slots, columns = tokens.shape
    blocks = bin_slots // BLK
    assert blocks == n and n % nz == 0 and n % 2 == 0
    here = n // nz
    shard = first_gain.shape[0]
    d = shard * n
    head_size = attention_bias.shape[2] * n
    heads_z = attention_bias.shape[1]
    heads = H // n
    width = heads * head_size
    units_z = up_weight.shape[1]
    units = units_z // n
    even_heads = heads_z % n == 0

    small = [first_gain, first_shift, out_bias, second_gain, second_shift, down_bias]
    small = small + [attention_bias.reshape(-1), up_bias.reshape(-1)]
    small = small + [t.astype(bf16) for t in (source_block, target_block, block_fill, block_start)]
    packed = small_gather(jnp.concatenate(small))
    at = 6 * shard
    vectors = packed[:, :at].reshape(n, 6, shard).transpose(1, 0, 2).reshape(6, 1, d).astype(f32)
    gain_one, shift_one, out_shift, gain_two, shift_two, down_shift = [vectors[i] for i in range(6)]
    size = attention_bias.size
    bias_z = packed[:, at : at + size].reshape(n, 2, heads_z, head_size // n)
    bias_z = bias_z.transpose(1, 2, 0, 3).reshape(2, heads_z * head_size)
    at = at + size
    size = up_bias.size
    up_z = packed[:, at : at + size].reshape(n, up_bias.shape[0], up_bias.shape[1])
    up_z = up_z.transpose(1, 0, 2).reshape(n, units)
    tables = packed[:, at + size :].reshape(n, 4, blocks).transpose(1, 0, 2).astype(jnp.int32)
    source, target, fill, start = [tables[i] for i in range(4)]
    if even_heads:
        bias_z = lax.dynamic_slice_in_dim(bias_z, p * (width // nz), width // nz, 1)
        head_ids = jnp.arange(nz, dtype=jnp.int32)[:, None] * heads_z + p * (heads_z // n)
        head_ids = (head_ids + jnp.arange(heads_z // n, dtype=jnp.int32)[None, :]).reshape(-1)
    else:
        head_ids = p * heads + jnp.arange(heads, dtype=jnp.int32)
    up_z = lax.dynamic_index_in_dim(up_z, p, 0, keepdims=False)
    bias_size = bias_z.size
    both_z = jnp.concatenate([bias_z.reshape(-1), up_z])
    every = jnp.zeros((nz, both_z.shape[0]), bf16)
    for r in range(nz):
        piece = turn(both_z, r) if r else both_z
        every = lax.dynamic_update_slice(every, piece[None], ((z - r) % nz, 0))
    mine = every[:, :bias_size].reshape(nz, 2, -1).transpose(1, 0, 2).reshape(2, -1)
    if not even_heads:
        mine = lax.dynamic_slice_in_dim(mine, p * width, width, 1)
    qkv_bias = jnp.concatenate([mine[0], jnp.zeros((width,), bf16), mine[1]]).astype(f32)[None]
    up_shift = every[:, bias_size:].reshape(1, nz * units).astype(f32)
    slopes = jnp.exp2(-8.0 * (head_ids + 1).astype(f32) / H)

    def spread_out(value, split, join):
        return lax.all_to_all(value, "dp", split_axis=split, concat_axis=join, tiled=True)

    def over_bins(value, axis):
        return lax.all_gather(value, "tensor", axis=axis, tiled=True)

    wanted = lax.dynamic_index_in_dim(source, p, 1, keepdims=False)
    near, far = plane_gather(tokens)
    out_weight, up_weight, down_weight, cotangent = after(
        (attention_out, up_weight, down_weight, cotangent), (near, far)
    )
    rows_in = to_bins(pick_blocks(near, far, wanted // blocks, wanted % blocks, blocks), here)
    near, far = plane_gather(after(cotangent, rows_in))
    grad_in = to_bins(pick_blocks(near, far, wanted // blocks, wanted % blocks, blocks), here)

    if even_heads:
        in_rows = over_bins(spread_out(attention_in.transpose(0, 2, 1), 1, 2), 1)
        out_rows = over_bins(spread_out(out_weight, 0, 1), 0)
    else:
        in_rows = spread_out(over_bins(attention_in, 2).transpose(0, 2, 1), 1, 2)
        out_rows = spread_out(over_bins(out_weight, 0), 0, 1)
    in_rows = in_rows.reshape(3 * width, d)
    up_part = over_bins(spread_out(up_weight, 1, 0), 1)
    down_part = over_bins(spread_out(down_weight, 0, 1), 0)

    first_bin = z * here
    kinds = near_kinds() + [k + 1 for k in near_kinds()]
    where = jnp.array(kinds, jnp.int32) ^ p
    single = bin_slots == MAXLEN
    offset = jnp.arange(bin_slots, dtype=jnp.int32) % BLK
    block_of = jnp.arange(bin_slots, dtype=jnp.int32) // BLK

    def bin_tables(g):
        bin_start = lax.dynamic_index_in_dim(start, first_bin + g, 0, keepdims=False)
        bin_fill = lax.dynamic_index_in_dim(fill, first_bin + g, 0, keepdims=False)
        segment = spread(bin_start)
        valid = offset < spread(bin_fill)
        place = (block_of - segment) * BLK + offset
        valid_rows = jnp.arange(BLK, dtype=jnp.int32) < lax.dynamic_index_in_dim(bin_fill, p, 0)
        return segment, place, valid, valid_rows[:, None]

    inverse = [kinds.index(k) for k in range(n)]
    order = jnp.array(inverse, jnp.int32)[jnp.arange(n, dtype=jnp.int32) ^ p]

    def split_rows(rows):
        back = jnp.take(rows.reshape(n, BLK, -1), where, axis=0).reshape(rows.shape)
        return back[: bin_slots // 2], back[bin_slots // 2 :]

    def attend(near, far, g):
        if single:
            return attend_one(near, far, where, slopes, heads, head_size)
        segment, place, valid, _ = bin_tables(g)
        rows = reorder(near, far, order)
        query, keys, values = rows[:, :width], rows[:, width : 2 * width], rows[:, 2 * width :]
        return split_rows(
            attend_any(query, keys, values, segment, place, valid, slopes, heads, head_size)
        )

    def attend_back(near, far, grad_near, grad_far, g):
        if single:
            return attend_one_back(near, far, grad_near, grad_far, where, slopes, heads, head_size)
        segment, place, valid, _ = bin_tables(g)
        rows = reorder(near, far, order)
        grad = reorder(grad_near, grad_far, order)
        query, keys, values = rows[:, :width], rows[:, width : 2 * width], rows[:, 2 * width :]
        return split_rows(
            attend_any_back(query, keys, values, grad, segment, place, valid, slopes, heads, head_size)
        )

    streams = []
    for g in range(here):
        s = {}
        s["valid"] = bin_tables(g)[3]
        s["x"] = rows_in[g].astype(f32)
        s["grad"] = jnp.where(s["valid"], grad_in[g].astype(f32), 0.0)
        s["unit_one"], s["scale_one"] = normalize(s["x"])
        norm_one = (s["unit_one"] * gain_one + shift_one).astype(bf16)
        s["one"] = plane_gather(norm_one)
        s["qkv"] = [(contract(v, in_rows, 1, 1) + qkv_bias).astype(bf16) for v in s["one"]]
        s["att"] = attend(*s["qkv"], g)
        resid = s["x"] + plane_sum(*s["att"], out_rows, 0) + out_shift
        s["unit_two"], s["scale_two"] = normalize(resid)
        norm_two = (s["unit_two"] * gain_two + shift_two).astype(bf16)
        s["two"] = plane_gather(norm_two)
        s["hidden"], s["slope"] = [], []
        for v in s["two"]:
            before = jnp.dot(v, up_part, preferred_element_type=f32) + up_shift
            share = 0.5 * (1.0 + lax.erf(before * root_half))
            s["hidden"].append((before * share).astype(bf16))
            density = jnp.exp(-0.5 * before * before) * density_scale
            s["slope"].append((share + before * density).astype(bf16))
        s["resid"] = resid
        s["branch"] = plane_gather(s["grad"].astype(bf16))
        streams.append(s)

    def pairs_sum(left, right):
        a = jnp.concatenate([v for s in streams for v in s[left]], axis=0)
        b = jnp.concatenate([v for s in streams for v in s[right]], axis=0)
        return contract(a, b, 0, 0)

    down_grad = pairs_sum("hidden", "branch").astype(bf16)
    branches = after([s["branch"] for s in streams], down_grad)
    down_grad = lax.psum_scatter(down_grad, "tensor", scatter_dimension=0, tiled=True)
    down_grad = spread_out(down_grad, 1, 0).astype(f32)
    for s, branch in zip(streams, branches):
        s["before"] = [
            (contract(v, down_part, 1, 1) * slope.astype(f32)).astype(bf16)
            for v, slope in zip(branch, s["slope"])
        ]
    up_grad = pairs_sum("two", "before").astype(bf16)
    up_grad = lax.psum_scatter(up_grad, "tensor", scatter_dimension=1, tiled=True)
    up_grad = spread_out(up_grad, 0, 1).astype(f32)
    up_bias_grad = sum(jnp.sum(v.astype(f32), axis=0) for s in streams for v in s["before"])
    for g, s in enumerate(streams):
        grad_two = plane_sum(*s["before"], up_part, 1)
        s["gain_two"] = jnp.sum(grad_two * s["unit_two"], axis=0)
        s["shift_two"] = jnp.sum(grad_two, axis=0)
        s["grad_resid"] = s["grad"] + norm_back(grad_two, s["unit_two"], s["scale_two"], gain_two)
        s["attn"] = plane_gather(s["grad_resid"].astype(bf16))
        grad_att = [contract(v, out_rows, 1, 1).astype(bf16) for v in s["attn"]]
        s["grad_qkv"] = attend_back(*s["qkv"], *grad_att, g)
    results = []
    for s in streams:
        result = s["resid"] + plane_sum(*s["hidden"], down_part, 0) + down_shift
        results.append(jnp.where(s["valid"], result, 0.0).astype(bf16))
    output = from_bins(jnp.stack(results))
    out_grad = pairs_sum("att", "attn").astype(bf16)
    if even_heads:
        out_grad = lax.psum_scatter(out_grad, "tensor", scatter_dimension=0, tiled=True)
        out_grad = spread_out(out_grad, 1, 0).astype(f32)
    else:
        out_grad = spread_out(out_grad, 1, 0)
        out_grad = lax.psum_scatter(out_grad, "tensor", scatter_dimension=0, tiled=True).astype(f32)
    in_grad = pairs_sum("grad_qkv", "one").astype(bf16).reshape(3, width, d)
    if even_heads:
        in_grad = in_grad.reshape(3, nz, width // nz, d).transpose(1, 0, 2, 3).reshape(-1, d)
        in_grad = lax.psum_scatter(in_grad, "tensor", scatter_dimension=0, tiled=True)
        in_grad = spread_out(in_grad.reshape(3, width // nz, d), 2, 1)
    else:
        in_grad = spread_out(in_grad, 2, 1)
        in_grad = lax.psum_scatter(in_grad, "tensor", scatter_dimension=1, tiled=True)
    in_grad = in_grad.transpose(0, 2, 1).astype(f32)
    bias_grad = sum(jnp.sum(v.astype(f32), axis=0) for s in streams for v in s["grad_qkv"])
    bias_grad = jnp.stack([bias_grad[:width], bias_grad[2 * width :]])

    input_rows = []
    for s in streams:
        grad_one = plane_sum(*s["grad_qkv"], in_rows, 0)
        s["gain_one"] = jnp.sum(grad_one * s["unit_one"], axis=0)
        s["shift_one"] = jnp.sum(grad_one, axis=0)
        grad_x = s["grad_resid"] + norm_back(grad_one, s["unit_one"], s["scale_one"], gain_one)
        input_rows.append(grad_x.astype(bf16))
    input_grad = from_bins(jnp.stack(input_rows))

    wanted = lax.dynamic_index_in_dim(target, p, 0, keepdims=False)

    def to_anchor(blocks_here):
        near, far = plane_gather(blocks_here.reshape(n * BLK, columns))
        return pick_blocks(near, far, wanted % blocks, wanted // blocks, n).reshape(bin_slots, columns)

    output = to_anchor(output)
    input_grad = to_anchor(input_grad)

    def over_streams(name):
        return sum(s[name] for s in streams)

    vectors = jnp.stack(
        [
            over_streams("gain_one"),
            over_streams("shift_one"),
            sum(jnp.sum(s["grad_resid"], axis=0) for s in streams),
            over_streams("gain_two"),
            over_streams("shift_two"),
            sum(jnp.sum(s["grad"], axis=0) for s in streams),
        ]
    ).reshape(6, n, shard).transpose(1, 0, 2).reshape(n, -1)
    if even_heads:
        bias_full = jnp.zeros((2, nz, n, width // nz), f32)
        bias_full = lax.dynamic_update_slice(
            bias_full, bias_grad.reshape(2, nz, 1, width // nz), (0, 0, p, 0)
        )
    else:
        bias_full = jnp.zeros((2, n, width), f32)
        bias_full = lax.dynamic_update_slice(bias_full, bias_grad.reshape(2, 1, width), (0, p, 0))
    bias_full = bias_full.reshape(2, nz, heads_z * n, head_size // n)
    up_full = jnp.zeros((nz, n, units), f32)
    up_full = lax.dynamic_update_slice(up_full, up_bias_grad.reshape(nz, 1, units), (0, p, 0))
    rows_z = up_bias.shape[0]
    bias_full = bias_full.reshape(2, nz, heads_z, n, head_size // n).transpose(1, 3, 0, 2, 4)
    up_full = up_full.reshape(nz, rows_z, n, up_bias.shape[1]).transpose(0, 2, 1, 3)
    by_slice = jnp.concatenate([bias_full.reshape(nz, n, -1), up_full.reshape(nz, n, -1)], axis=2)

    def for_slice(r):
        return jnp.concatenate(
            [vectors, lax.dynamic_index_in_dim(by_slice, (z + r) % nz, 0, keepdims=False)], axis=1
        )

    table = for_slice(0)
    for r in range(1, nz):
        table = table + turn(for_slice(r), r)
    mine = lax.dynamic_index_in_dim(table, p, 0, keepdims=False)
    for k in range(1, n):
        mine = mine + swap(lax.dynamic_index_in_dim(table, p ^ k, 0, keepdims=False), k)
    vectors = mine[: 6 * shard].reshape(6, shard)
    at = 6 * shard + attention_bias.size
    bias_grad = mine[6 * shard : at].reshape(attention_bias.shape)
    up_bias_grad = mine[at:].reshape(up_bias.shape)
    return (
        output,
        input_grad,
        vectors[0],
        vectors[1],
        in_grad,
        bias_grad,
        out_grad,
        vectors[2],
        vectors[3],
        vectors[4],
        up_grad,
        up_bias_grad,
        down_grad,
        vectors[5],
    )


def solution(mesh):
    return jax.shard_map(
        on_device,
        mesh=mesh,
        in_specs=(
            P("dp", "tensor"),
            P("dp", "tensor"),
            P("dp"),
            P("dp"),
            P(None, "dp", "tensor"),
            P(None, "tensor", "dp"),
            P("tensor", "dp"),
            P("dp"),
            P("dp"),
            P("dp"),
            P("dp", "tensor"),
            P("tensor", "dp"),
            P("tensor", "dp"),
            P("dp"),
            P("dp"),
            P("dp"),
            P("dp"),
            P("dp"),
        ),
        out_specs=(
            P("dp", "tensor"),
            P("dp", "tensor"),
            P("dp"),
            P("dp"),
            P(None, "dp", "tensor"),
            P(None, "tensor", "dp"),
            P("tensor", "dp"),
            P("dp"),
            P("dp"),
            P("dp"),
            P("dp", "tensor"),
            P("tensor", "dp"),
            P("tensor", "dp"),
            P("dp"),
        ),
        check_vma=False,
    )
```

```python
import jax
import jax.numpy as jnp
from jax import lax
from jax.experimental import pallas as pl
from jax.experimental.pallas import tpu as pltpu
from jax.sharding import PartitionSpec as P


H = 32
BLK = 128
MAXLEN = 1024
QB = 512
TILE = 256

norm_eps = 1e-05
masked_score = -1e30
density_scale = 0.3989422804014327
root_half = 0.7071067811865476

f32 = jnp.float32
bf16 = jnp.bfloat16


def normalize(rows):
    mean = jnp.mean(rows, axis=-1, keepdims=True)
    centred = rows - mean
    variance = jnp.mean(centred * centred, axis=-1, keepdims=True)
    scale = lax.rsqrt(variance + norm_eps)
    return (centred * scale, scale)


def norm_back(grad_norm, unit, scale, gain):
    grad_unit = grad_norm * gain
    mean_grad = jnp.mean(grad_unit, axis=-1, keepdims=True)
    mean_dot = jnp.mean(grad_unit * unit, axis=-1, keepdims=True)
    return scale * (grad_unit - mean_grad - unit * mean_dot)


def spread(table):
    return jnp.broadcast_to(table[:, None], (table.shape[0], BLK)).reshape(-1)


def swap(value, k):
    count = lax.axis_size("dp")
    return lax.ppermute(value, "dp", [(i, i ^ k) for i in range(count)])


def turn(value, r):
    count = lax.axis_size("tensor")
    return lax.ppermute(value, "tensor", [(i, (i + r) % count) for i in range(count)])


def after(values, others):
    return lax.optimization_barrier((values, others))[0]


def near_order(bins):
    count = lax.axis_size("dp")
    if count == 8 and bins == 2:
        return [(0, 0), (0, 1), (2, 1), (2, 0), (6, 0), (6, 1), (4, 1), (4, 0)]
    return [(k, b) for k in range(0, count, 2) for b in range(bins)]


def plane_gather(rows, bins):
    if lax.axis_size("dp") == 8 and bins == 2:
        half = rows.shape[0] // 2
        a = swap(rows, 2)
        b = swap(rows, 4)
        c = swap(a[:half], 4)
        d = swap(b[half:], 2)
        pieces = [rows, a[half:], a[:half], c, d, b[half:], b[:half]]
    else:
        pieces = [swap(rows, k) if k else rows for k in range(0, lax.axis_size("dp"), 2)]
    near = jnp.concatenate(pieces, axis=0)
    return near, swap(near, 1)


def sum_pair(near, far, weight, dim):
    other = swap(contract(far, weight, 1, dim).astype(bf16), 1)
    return (contract(near, weight, 1, dim) + other.astype(f32)).astype(bf16)


def sum_first(both, bins):
    count = lax.axis_size("dp")
    step = both.shape[0] * 2 // count
    if count == 8 and bins == 2:
        half = step // 2
        return [swap(both[3 * half : 5 * half], 2), swap(both[5 * half : 7 * half], 4)]
    return [swap(both[j * step : (j + 1) * step], 2 * j) for j in range(1, count // 2)]


def sum_second(both, first, bins):
    if lax.axis_size("dp") == 8 and bins == 2:
        half = both.shape[0] // 8
        a, b = [v.astype(f32) for v in first]
        c = both[7 * half :].astype(f32) + a[half:]
        d = both[2 * half : 3 * half].astype(f32) + b[:half]
        return [swap(c.astype(bf16), 4), swap(d.astype(bf16), 2)]
    return []


def sum_last(both, first, second, bins):
    count = lax.axis_size("dp")
    step = both.shape[0] * 2 // count
    if count == 8 and bins == 2:
        half = step // 2
        (a, b), (c, d) = [[v.astype(f32) for v in pair] for pair in (first, second)]
        upper = both[:half].astype(f32) + a[:half] + c
        lower = both[half:step].astype(f32) + b[half:] + d
        return jnp.concatenate([upper, lower], axis=0)
    total = both[:step].astype(f32)
    for v in first:
        total = total + v.astype(f32)
    return total


def plane_sum(near, far, weight, dim, bins):
    both = sum_pair(near, far, weight, dim)
    first = sum_first(both, bins)
    second = sum_second(both, first, bins)
    return sum_last(both, first, second, bins)


def small_gather(value):
    count = lax.axis_size("dp")
    value = value.reshape(1, -1)
    k = 1
    while k < count:
        value = jnp.concatenate([value, swap(value, k)], axis=0)
        k *= 2
    return jnp.take(value, jnp.arange(count, dtype=jnp.int32) ^ lax.axis_index("dp"), axis=0)


def pick_blocks(rows, wanted):
    count = wanted.shape[0]

    def body(table, source, out):
        for i in range(count):
            begin = pl.multiple_of(table[i] * BLK, BLK)
            out[i * BLK : (i + 1) * BLK, :] = source[pl.ds(begin, BLK), :]

    return pl.pallas_call(
        body,
        out_shape=jax.ShapeDtypeStruct((count * BLK, rows.shape[1]), rows.dtype),
        in_specs=[smem(), vmem()],
        out_specs=vmem(),
        name="pick",
    )(wanted, rows)


def to_bins(pieces):
    count = lax.axis_size("tensor")
    z = lax.axis_index("tensor")
    wide = pieces[0].shape[-1]
    out = jnp.zeros((pieces[0].shape[0], wide * count), pieces[0].dtype)
    for r, piece in enumerate(pieces):
        if r:
            piece = turn(piece, r)
        out = lax.dynamic_update_slice(out, piece, (0, ((z - r) % count) * wide))
    return out


def from_bins(rows):
    count = lax.axis_size("tensor")
    z = lax.axis_index("tensor")
    wide = rows.shape[-1] // count
    pieces = []
    for r in range(count):
        piece = lax.dynamic_slice_in_dim(rows, ((z + r) % count) * wide, wide, 1)
        pieces.append(turn(piece, r) if r else piece)
    return jnp.concatenate(pieces, axis=0)


def contract(a, b, left, right):
    return lax.dot_general(a, b, (((left,), (right,)), ((), ())), preferred_element_type=f32)


def spread_blocks(bin_block):
    count = lax.axis_size("dp")
    edges = count * count
    levels = count.bit_length() - 1
    assert count == 1 << levels and bin_block.shape == (edges,)

    def body(bin_column, bin_row, color):
        column = lax.broadcasted_iota(jnp.int32, (edges, 1), 0)
        row = lax.broadcasted_iota(jnp.int32, (1, edges), 1)
        here_column, here_row = column, row
        there_column, there_row = bin_column[...], bin_row[...]
        for level in range(levels):
            half = 1 << (levels - level - 1)
            here = jnp.where((here_column ^ 1) == here_row, 1.0, 0.0).astype(bf16)
            there = jnp.where((there_column ^ 1) == there_row, 1.0, 0.0).astype(bf16)
            hop = contract(here, there, 1, 0).astype(bf16)
            least_column, least_row = column.astype(f32), row.astype(f32)
            for _ in range(2 * levels - 1):
                least_column = jnp.minimum(least_column, contract(hop, least_column.astype(bf16), 1, 0))
                least_row = jnp.minimum(least_row, contract(least_row.astype(bf16), hop, 1, 0))
                hop = contract(hop, hop, 1, 0).astype(bf16)
            bit_column = least_column > contract(here, least_column.astype(bf16), 1, 0)
            bit_row = least_row > contract(least_row.astype(bf16), here, 1, 0)

            def refine(key, bit):
                low = key & (2 * half - 1)
                return key - low + jnp.where(bit, half, 0) + (low >> 1)

            here_column, here_row = refine(here_column, bit_column), refine(here_row, bit_row)
            there_column, there_row = refine(there_column, bit_column), refine(there_row, bit_row)
        color[...] = here_row & (count - 1)

    color = pl.pallas_call(
        body, out_shape=jax.ShapeDtypeStruct((1, edges), jnp.int32), name="spread_blocks"
    )(bin_block.reshape(edges, 1), bin_block.reshape(1, edges))
    return color.reshape(count, count)


def attend_kernel(bins, heads, head_size, order, where, slopes, near, far, out_near, out_far, qkv, mixed):
    width = heads * head_size
    for j, b in enumerate(order):
        source, i = (near, j) if j < len(order) // 2 else (far, j - len(order) // 2)
        at = pl.multiple_of(where[j] * BLK, BLK)
        for part in range(3):
            for h in range(heads):
                lo = part * width + h * head_size
                piece = source[i * BLK : (i + 1) * BLK, lo : lo + head_size]
                if part == 0:
                    piece = (piece.astype(f32) * 0.125).astype(bf16)
                qkv[part, b * heads + h, pl.ds(at, BLK), :] = piece
    slots = qkv.shape[2]

    def one_head(h, carry):
        slope = slopes[h % heads]
        for t in range(slots // TILE):
            lo, hi = t * TILE, (t + 1) * TILE
            query = qkv[0, h, lo:hi, :]
            scores = contract(query, qkv[1, h, 0:hi, :], 1, 1)
            column = lax.broadcasted_iota(jnp.int32, (1, hi), 1)
            scores = scores + slope * (column - hi).astype(f32)
            diagonal = scores[:, lo:hi]
            rows = lax.broadcasted_iota(jnp.int32, (TILE, TILE), 0)
            columns = lax.broadcasted_iota(jnp.int32, (TILE, TILE), 1)
            diagonal = jnp.where(columns <= rows, diagonal, masked_score)
            scores = jnp.concatenate([scores[:, :lo], diagonal], axis=1) if t else diagonal
            top = jnp.max(scores, axis=1, keepdims=True)
            weights = jnp.exp(scores - top)
            total = jnp.sum(weights, axis=1, keepdims=True)
            result = contract(weights.astype(bf16), qkv[2, h, 0:hi, :], 1, 0) / total
            mixed[h, lo:hi, :] = result.astype(bf16)
        return carry

    lax.fori_loop(0, bins * heads, one_head, 0)
    for j, b in enumerate(order):
        target, i = (out_near, j) if j < len(order) // 2 else (out_far, j - len(order) // 2)
        at = pl.multiple_of(where[j] * BLK, BLK)
        for h in range(heads):
            target[i * BLK : (i + 1) * BLK, h * head_size : (h + 1) * head_size] = mixed[
                b * heads + h, pl.ds(at, BLK), :
            ]


def attend_back_kernel(
    bins, heads, head_size, order, where, slopes, near, far, grad_near, grad_far, out_near, out_far, qkvg, sums, parts
):
    width = heads * head_size
    for j, b in enumerate(order):
        near_half = j < len(order) // 2
        source, grad, i = (near, grad_near, j) if near_half else (far, grad_far, j - len(order) // 2)
        at = pl.multiple_of(where[j] * BLK, BLK)
        for part in range(4):
            for h in range(heads):
                lo = part * width + h * head_size
                if part < 3:
                    piece = source[i * BLK : (i + 1) * BLK, lo : lo + head_size]
                else:
                    piece = grad[i * BLK : (i + 1) * BLK, h * head_size : (h + 1) * head_size]
                if part == 0:
                    piece = (piece.astype(f32) * 0.125).astype(bf16)
                qkvg[part, b * heads + h, pl.ds(at, BLK), :] = piece
    slots = qkvg.shape[2]

    def one_head(h, carry):
        slope = slopes[h % heads]
        sums[...] = jnp.zeros_like(sums)
        for t in range(slots // TILE):
            lo, hi = t * TILE, (t + 1) * TILE
            query = qkvg[0, h, lo:hi, :]
            grad = qkvg[3, h, lo:hi, :]
            keys = qkvg[1, h, 0:hi, :]
            scores = contract(keys, query, 1, 1)
            key_place = lax.broadcasted_iota(jnp.int32, (hi, 1), 0)
            scores = scores + slope * (key_place - hi).astype(f32)
            diagonal = scores[lo:hi, :]
            rows = lax.broadcasted_iota(jnp.int32, (TILE, TILE), 0)
            columns = lax.broadcasted_iota(jnp.int32, (TILE, TILE), 1)
            diagonal = jnp.where(rows <= columns, diagonal, masked_score)
            scores = jnp.concatenate([scores[:lo, :], diagonal], axis=0) if t else diagonal
            top = jnp.max(scores, axis=0, keepdims=True)
            weights = jnp.exp(scores - top)
            total = jnp.sum(weights, axis=0, keepdims=True)
            probs = weights * (1.0 / total)
            grad_probs = contract(qkvg[2, h, 0:hi, :], grad, 1, 1)
            inner = jnp.sum(probs * grad_probs, axis=0, keepdims=True)
            grad_scores = (probs * (grad_probs - inner)).astype(bf16)
            sums[0, 0:hi, :] += contract(grad_scores, query, 1, 0)
            sums[1, 0:hi, :] += contract(probs.astype(bf16), grad, 1, 0)
            grad_query = contract(grad_scores, keys, 0, 0) * 0.125
            parts[0, h, lo:hi, :] = grad_query.astype(bf16)
        parts[1, h] = sums[0].astype(bf16)
        parts[2, h] = sums[1].astype(bf16)
        return carry

    lax.fori_loop(0, bins * heads, one_head, 0)
    for j, b in enumerate(order):
        target, i = (out_near, j) if j < len(order) // 2 else (out_far, j - len(order) // 2)
        at = pl.multiple_of(where[j] * BLK, BLK)
        for part in range(3):
            for h in range(heads):
                lo = part * width + h * head_size
                target[i * BLK : (i + 1) * BLK, lo : lo + head_size] = parts[
                    part, b * heads + h, pl.ds(at, BLK), :
                ]


def smem():
    return pl.BlockSpec(memory_space=pltpu.SMEM)


def vmem():
    return pl.BlockSpec(memory_space=pltpu.VMEM)


def attend_one(near, far, order, where, slopes, heads, head_size):
    bins = max(order) + 1
    slots = 2 * near.shape[0] // bins
    width = heads * head_size
    half = jax.ShapeDtypeStruct((near.shape[0], width), bf16)

    def body(*refs):
        attend_kernel(bins, heads, head_size, order, *refs)

    return pl.pallas_call(
        body,
        out_shape=(half, half),
        in_specs=[smem(), smem(), vmem(), vmem()],
        out_specs=(vmem(), vmem()),
        scratch_shapes=[
            pltpu.VMEM((3, bins * heads, slots, head_size), bf16),
            pltpu.VMEM((bins * heads, slots, head_size), bf16),
        ],
        cost_estimate=pl.CostEstimate(
            flops=2 * bins * slots * slots * width,
            transcendentals=bins * slots * slots * heads // 2,
            bytes_accessed=8 * bins * slots * width,
        ),
        name="attend",
    )(where, slopes, near, far)


def attend_one_back(near, far, grad_near, grad_far, order, where, slopes, heads, head_size):
    bins = max(order) + 1
    slots = 2 * near.shape[0] // bins
    width = heads * head_size
    half = jax.ShapeDtypeStruct(near.shape, bf16)

    def body(*refs):
        attend_back_kernel(bins, heads, head_size, order, *refs)

    return pl.pallas_call(
        body,
        out_shape=(half, half),
        in_specs=[smem(), smem(), vmem(), vmem(), vmem(), vmem()],
        out_specs=(vmem(), vmem()),
        scratch_shapes=[
            pltpu.VMEM((4, bins * heads, slots, head_size), bf16),
            pltpu.VMEM((2, slots, head_size), f32),
            pltpu.VMEM((3, bins * heads, slots, head_size), bf16),
        ],
        cost_estimate=pl.CostEstimate(
            flops=5 * bins * slots * slots * width,
            transcendentals=bins * slots * slots * heads // 2,
            bytes_accessed=16 * bins * slots * width,
        ),
        name="attend_back",
    )(where, slopes, near, far, grad_near, grad_far)


def block_view(query, keys, values, segment, place, valid, slopes, heads, head_size):
    width = heads * head_size
    keys_pad = jnp.concatenate([jnp.zeros((MAXLEN, width), bf16), keys])
    values_pad = jnp.concatenate([jnp.zeros((MAXLEN, width), bf16), values])
    segment_pad = jnp.concatenate([jnp.full((MAXLEN,), -1, jnp.int32), segment])
    place_pad = jnp.concatenate([jnp.zeros((MAXLEN,), jnp.int32), place])
    valid_pad = jnp.concatenate([jnp.zeros((MAXLEN,), dtype=bool), valid])
    window = QB + MAXLEN

    def block_scores(begin):
        query_block = lax.dynamic_slice_in_dim(query, begin, QB).reshape(QB, heads, head_size)
        key_block = lax.dynamic_slice_in_dim(keys_pad, begin, window).reshape(window, heads, head_size)
        value_block = lax.dynamic_slice_in_dim(values_pad, begin, window).reshape(window, heads, head_size)
        query_segment = lax.dynamic_slice_in_dim(segment, begin, QB)
        query_place = lax.dynamic_slice_in_dim(place, begin, QB)
        key_segment = lax.dynamic_slice_in_dim(segment_pad, begin, window)
        key_place = lax.dynamic_slice_in_dim(place_pad, begin, window)
        key_valid = lax.dynamic_slice_in_dim(valid_pad, begin, window)
        raw = jnp.einsum("qhe,khe->hqk", query_block, key_block, preferred_element_type=f32) * 0.125
        distance = (query_place[:, None] - key_place[None, :]).astype(f32)
        raw = raw - slopes[:, None, None] * distance[None]
        allowed = (
            (query_segment[:, None] == key_segment[None, :])
            & (key_place[None, :] <= query_place[:, None])
            & key_valid[None, :]
        )
        return (jnp.where(allowed[None], raw, masked_score), query_block, key_block, value_block)

    return block_scores, window


def attend_any(query, keys, values, segment, place, valid, slopes, heads, head_size):
    slots, width = query.shape
    block_scores, _ = block_view(query, keys, values, segment, place, valid, slopes, heads, head_size)

    def forward_block(index, attended):
        begin = index * QB
        scores, _, _, value_block = block_scores(begin)
        weights = jax.nn.softmax(scores, axis=-1).astype(bf16)
        mixed = jnp.einsum("hqk,khe->qhe", weights, value_block, preferred_element_type=f32)
        return lax.dynamic_update_slice_in_dim(attended, mixed.reshape(QB, width).astype(bf16), begin, 0)

    return lax.fori_loop(0, slots // QB, forward_block, jnp.zeros((slots, width), bf16))


def attend_any_back(query, keys, values, grad, segment, place, valid, slopes, heads, head_size):
    slots, width = query.shape
    block_scores, window = block_view(query, keys, values, segment, place, valid, slopes, heads, head_size)

    def backward_block(index, carry):
        grad_query, grad_keys, grad_values = carry
        begin = index * QB
        scores, query_block, key_block, value_block = block_scores(begin)
        probs = jax.nn.softmax(scores, axis=-1)
        grad_block = lax.dynamic_slice_in_dim(grad, begin, QB).reshape(QB, heads, head_size)
        grad_probs = jnp.einsum("qhe,khe->hqk", grad_block, value_block, preferred_element_type=f32)
        inner = jnp.sum(probs * grad_probs, axis=-1, keepdims=True)
        grad_scores = (probs * (grad_probs - inner)).astype(bf16)
        query_part = jnp.einsum("hqk,khe->qhe", grad_scores, key_block, preferred_element_type=f32) * 0.125
        key_part = jnp.einsum("hqk,qhe->khe", grad_scores, query_block, preferred_element_type=f32) * 0.125
        value_part = jnp.einsum("hqk,qhe->khe", probs.astype(bf16), grad_block, preferred_element_type=f32)
        grad_query = lax.dynamic_update_slice_in_dim(grad_query, query_part.reshape(QB, width), begin, 0)
        old_keys = lax.dynamic_slice_in_dim(grad_keys, begin, window)
        grad_keys = lax.dynamic_update_slice_in_dim(
            grad_keys, old_keys + key_part.reshape(window, width), begin, 0
        )
        old_values = lax.dynamic_slice_in_dim(grad_values, begin, window)
        grad_values = lax.dynamic_update_slice_in_dim(
            grad_values, old_values + value_part.reshape(window, width), begin, 0
        )
        return (grad_query, grad_keys, grad_values)

    padded_zero = jnp.zeros((MAXLEN + slots, width), f32)
    grad_query, grad_keys, grad_values = lax.fori_loop(
        0, slots // QB, backward_block, (jnp.zeros((slots, width), f32), padded_zero, padded_zero)
    )
    return jnp.concatenate([grad_query, grad_keys[MAXLEN:], grad_values[MAXLEN:]], axis=1).astype(bf16)


def on_device(
    tokens,
    cotangent,
    first_gain,
    first_shift,
    attention_in,
    attention_bias,
    attention_out,
    out_bias,
    second_gain,
    second_shift,
    up_weight,
    up_bias,
    down_weight,
    down_bias,
    source_block,
    target_block,
    block_fill,
    block_start,
):
    n = lax.axis_size("dp")
    nz = lax.axis_size("tensor")
    p = lax.axis_index("dp")
    z = lax.axis_index("tensor")
    bin_slots, _ = tokens.shape
    blocks = bin_slots // BLK
    assert blocks == n and n % nz == 0 and n % 2 == 0
    here = n // nz
    shard = first_gain.shape[0]
    d = shard * n
    head_size = attention_bias.shape[2] * n
    heads_z = attention_bias.shape[1]
    heads = H // n
    width = heads * head_size
    units_z = up_weight.shape[1]
    units = units_z // n
    even_heads = heads_z % n == 0

    small = [first_gain, first_shift, out_bias, second_gain, second_shift, down_bias]
    small = small + [attention_bias.reshape(-1), up_bias.reshape(-1)]
    small = small + [t.astype(bf16) for t in (target_block, block_fill, block_start)]
    packed = small_gather(jnp.concatenate(small))
    at = 6 * shard
    vectors = packed[:, :at].reshape(n, 6, shard).transpose(1, 0, 2).reshape(6, 1, d).astype(f32)
    gain_one, shift_one, out_shift, gain_two, shift_two, down_shift = [vectors[i] for i in range(6)]
    size = attention_bias.size
    bias_z = packed[:, at : at + size].reshape(n, 2, heads_z, head_size // n)
    bias_z = bias_z.transpose(1, 2, 0, 3).reshape(2, heads_z * head_size)
    at = at + size
    size = up_bias.size
    up_z = packed[:, at : at + size].reshape(n, up_bias.shape[0], up_bias.shape[1])
    up_z = up_z.transpose(1, 0, 2).reshape(n, units)
    tables = packed[:, at + size :].reshape(n, 3, blocks).transpose(1, 0, 2).astype(jnp.int32)
    target, fill, start = [tables[i] for i in range(3)]
    if even_heads:
        bias_z = lax.dynamic_slice_in_dim(bias_z, p * (width // nz), width // nz, 1)
        head_ids = jnp.arange(nz, dtype=jnp.int32)[:, None] * heads_z + p * (heads_z // n)
        head_ids = (head_ids + jnp.arange(heads_z // n, dtype=jnp.int32)[None, :]).reshape(-1)
    else:
        head_ids = p * heads + jnp.arange(heads, dtype=jnp.int32)
    up_z = lax.dynamic_index_in_dim(up_z, p, 0, keepdims=False)
    bias_size = bias_z.size
    both_z = jnp.concatenate([bias_z.reshape(-1), up_z])
    every = jnp.zeros((nz, both_z.shape[0]), bf16)
    for r in range(nz):
        piece = turn(both_z, r) if r else both_z
        every = lax.dynamic_update_slice(every, piece[None], ((z - r) % nz, 0))
    mine = every[:, :bias_size].reshape(nz, 2, -1).transpose(1, 0, 2).reshape(2, -1)
    if not even_heads:
        mine = lax.dynamic_slice_in_dim(mine, p * width, width, 1)
    qkv_bias = jnp.concatenate([mine[0], jnp.zeros((width,), bf16), mine[1]]).astype(f32)[None]
    up_shift = every[:, bias_size:].reshape(1, nz * units).astype(f32)
    slopes = jnp.exp2(-8.0 * (head_ids + 1).astype(f32) / H)

    def spread_out(value, split, join):
        return lax.all_to_all(value, "dp", split_axis=split, concat_axis=join, tiled=True)

    def over_bins(value, axis):
        return lax.all_gather(value, "tensor", axis=axis, tiled=True)

    if even_heads:
        in_rows = over_bins(spread_out(attention_in.transpose(0, 2, 1), 1, 2), 1)
    else:
        in_rows = spread_out(over_bins(attention_in, 2).transpose(0, 2, 1), 1, 2)
    in_rows = in_rows.reshape(3 * width, d)
    first_bin = z * here
    ranks = jnp.arange(n, dtype=jnp.int32)
    color = spread_blocks(target.reshape(-1))
    match = color[:, :, None] == ranks[None, None, :]
    held = jnp.sum(jnp.where(match, target[:, :, None], 0), axis=1)
    color = lax.dynamic_index_in_dim(color, p, 0, keepdims=False)
    leave = jnp.sum(jnp.where(color[:, None] == ranks[None, :], ranks[:, None], 0), axis=0)
    held_bin = lax.dynamic_index_in_dim(held // blocks, p, 1, keepdims=False)
    held_by = jnp.sum(jnp.where(held_bin[:, None] == ranks[None, :], ranks[:, None], 0), axis=0)

    ahead = (first_bin + ranks) % n
    at_ahead = held_by[ahead]
    behind = (first_bin + here - 1 - ranks // here * here) % n
    behind = behind - (here - 1) + ranks % here
    place_of = jnp.sum(jnp.where(behind[None, :] == held_bin[:, None], ranks[None, :], 0), axis=1)

    def bring(rows):
        rows = spread_out(pick_blocks(rows, leave), 0, 0)
        return pick_blocks(rows, at_ahead)

    def bring_on(rows):
        return to_bins(jnp.split(rows, nz, axis=0))

    def take_back(rows):
        return spread_out(pick_blocks(from_bins(rows), place_of), 0, 0)

    rows_in = bring(tokens)
    cotangent = after(cotangent, rows_in)
    rows_in = bring_on(rows_in)
    if even_heads:
        out_rows = over_bins(spread_out(attention_out, 0, 1), 0)
    else:
        out_rows = spread_out(over_bins(attention_out, 0), 0, 1)
    up_part = over_bins(spread_out(up_weight, 1, 0), 1)
    down_part = over_bins(spread_out(down_weight, 0, 1), 0)
    grad_in = bring(cotangent)

    gathered = near_order(here)
    gathered = gathered + [(k + 1, b) for k, b in gathered]
    order = [b for _, b in gathered]
    of_bin = [held // blocks == first_bin + g for g in range(here)]
    slot_of = jnp.stack([jnp.sum(jnp.where(match, held % blocks, 0), axis=0) for match in of_bin])
    where = slot_of[jnp.array(order), jnp.array([k for k, _ in gathered], jnp.int32) ^ p]
    single = bin_slots == MAXLEN
    offset = jnp.arange(bin_slots, dtype=jnp.int32) % BLK
    block_of = jnp.arange(bin_slots, dtype=jnp.int32) // BLK

    def bin_tables(g):
        bin_start = lax.dynamic_index_in_dim(start, first_bin + g, 0, keepdims=False)
        bin_fill = lax.dynamic_index_in_dim(fill, first_bin + g, 0, keepdims=False)
        segment = spread(bin_start)
        valid = offset < spread(bin_fill)
        place = (block_of - segment) * BLK + offset
        slot = lax.dynamic_index_in_dim(slot_of[g], p, 0, keepdims=False)
        valid_rows = jnp.arange(BLK, dtype=jnp.int32) < lax.dynamic_index_in_dim(bin_fill, slot, 0)
        return segment, place, valid, valid_rows

    sort_key = where + n * jnp.array(order, jnp.int32)
    unsorted = jnp.argsort(sort_key)

    def by_bin(near, far):
        rows = jnp.concatenate([near, far], axis=0).reshape(here * n, BLK, -1)
        return jnp.take(rows, unsorted, axis=0).reshape(here, bin_slots, -1)

    def as_gathered(rows):
        rows = jnp.take(rows.reshape(here * n, BLK, -1), sort_key, axis=0)
        rows = rows.reshape(here * bin_slots, -1)
        return rows[: here * bin_slots // 2], rows[here * bin_slots // 2 :]

    def attend(near, far):
        if single:
            return attend_one(near, far, order, where, slopes, heads, head_size)
        rows = by_bin(near, far)
        mixed = []
        for g in range(here):
            query, keys, values = jnp.split(rows[g], 3, axis=1)
            tables = bin_tables(g)[:3]
            mixed.append(attend_any(query, keys, values, *tables, slopes, heads, head_size))
        return as_gathered(jnp.stack(mixed))

    def attend_back(near, far, grad_near, grad_far):
        if single:
            return attend_one_back(near, far, grad_near, grad_far, order, where, slopes, heads, head_size)
        rows = by_bin(near, far)
        grad = by_bin(grad_near, grad_far)
        grads = []
        for g in range(here):
            query, keys, values = jnp.split(rows[g], 3, axis=1)
            tables = bin_tables(g)[:3]
            grads.append(
                attend_any_back(query, keys, values, grad[g], *tables, slopes, heads, head_size)
            )
        return as_gathered(jnp.stack(grads))

    valid = jnp.concatenate([bin_tables(g)[3] for g in range(here)])[:, None]
    x = rows_in.astype(f32)
    unit_one, scale_one = normalize(x)
    one = plane_gather((unit_one * gain_one + shift_one).astype(bf16), here)
    one = after(one, grad_in)
    grad_in = bring_on(grad_in)
    qkv = [(contract(v, in_rows, 1, 1) + qkv_bias).astype(bf16) for v in one]
    att = attend(*after(qkv, grad_in))
    grad = jnp.where(valid, grad_in.astype(f32), 0.0)
    branch = plane_gather(grad.astype(bf16), here)
    resid = x + plane_sum(*att, out_rows, 0, here) + out_shift
    unit_two, scale_two = normalize(resid)
    norm_two = (unit_two * gain_two + shift_two).astype(bf16)
    two = plane_gather(norm_two, here)
    hidden, slope = [], []
    for v in two:
        before = jnp.dot(v, up_part, preferred_element_type=f32) + up_shift
        share = 0.5 * (1.0 + lax.erf(before * root_half))
        hidden.append((before * share).astype(bf16))
        density = jnp.exp(-0.5 * before * before) * density_scale
        slope.append((share + before * density).astype(bf16))

    def pairs_sum(left, right):
        a = jnp.concatenate(left, axis=0)
        b = jnp.concatenate(right, axis=0)
        return contract(a, b, 0, 0).astype(bf16)

    down_sum = pairs_sum(hidden, branch)
    down_grad = lax.psum_scatter(down_sum, "tensor", scatter_dimension=0, tiled=True)
    down_grad = spread_out(down_grad, 1, 0).astype(f32)
    grad_before = [
        (contract(v, down_part, 1, 1) * w.astype(f32)).astype(bf16) for v, w in zip(branch, slope)
    ]
    up_sum = pairs_sum(two, grad_before)
    up_grad = lax.psum_scatter(up_sum, "tensor", scatter_dimension=1, tiled=True)
    up_grad = spread_out(up_grad, 0, 1).astype(f32)
    up_bias_grad = sum(jnp.sum(v.astype(f32), axis=0) for v in grad_before)
    grad_two = plane_sum(*grad_before, up_part, 1, here)
    grad_resid = grad + norm_back(grad_two, unit_two, scale_two, gain_two)
    attn = plane_gather(after(grad_resid.astype(bf16), down_sum), here)
    out_grad = pairs_sum(att, attn)
    grad_att = [contract(v, out_rows, 1, 1).astype(bf16) for v in attn]
    both_out = sum_pair(*after(hidden, attn), down_part, 0)
    first_out = sum_first(both_out, here)
    grad_att = after(grad_att, (up_sum, out_grad, down_grad, both_out))
    grad_qkv = attend_back(*qkv, *grad_att)
    grad_qkv, first_out = lax.optimization_barrier((grad_qkv, first_out))
    second_out = sum_second(both_out, first_out, here)
    if even_heads:
        out_grad = lax.psum_scatter(out_grad, "tensor", scatter_dimension=0, tiled=True)
        out_grad = spread_out(out_grad, 1, 0).astype(f32)
    else:
        out_grad = spread_out(out_grad, 1, 0)
        out_grad = lax.psum_scatter(out_grad, "tensor", scatter_dimension=0, tiled=True).astype(f32)
    both_one = sum_pair(*grad_qkv, in_rows, 0)
    first_one = sum_first(both_one, here)
    result = resid + sum_last(both_out, first_out, second_out, here) + down_shift
    result = jnp.where(valid, result, 0.0).astype(bf16)
    output = pick_blocks(take_back(result), color)
    in_grad = pairs_sum(grad_qkv, one).reshape(3, width, d)
    if even_heads:
        in_grad = in_grad.reshape(3, nz, width // nz, d).transpose(1, 0, 2, 3).reshape(-1, d)
        in_grad = lax.psum_scatter(in_grad, "tensor", scatter_dimension=0, tiled=True)
        in_grad = spread_out(in_grad.reshape(3, width // nz, d), 2, 1)
    else:
        in_grad = spread_out(in_grad, 2, 1)
        in_grad = lax.psum_scatter(in_grad, "tensor", scatter_dimension=1, tiled=True)
    in_grad = in_grad.transpose(0, 2, 1).astype(f32)
    bias_grad = sum(jnp.sum(v.astype(f32), axis=0) for v in grad_qkv)
    bias_grad = jnp.stack([bias_grad[:width], bias_grad[2 * width :]])
    first_one = after(first_one, result)
    second_one = sum_second(both_one, first_one, here)
    grad_one = sum_last(both_one, first_one, second_one, here)
    input_rows = grad_resid + norm_back(grad_one, unit_one, scale_one, gain_one)
    input_grad = take_back(after(input_rows.astype(bf16), (up_grad, out_grad)))
    input_grad = pick_blocks(after(input_grad, in_grad), color)

    vectors = jnp.stack(
        [
            jnp.sum(grad_one * unit_one, axis=0),
            jnp.sum(grad_one, axis=0),
            jnp.sum(grad_resid, axis=0),
            jnp.sum(grad_two * unit_two, axis=0),
            jnp.sum(grad_two, axis=0),
            jnp.sum(grad, axis=0),
        ]
    ).reshape(6, n, shard).transpose(1, 0, 2).reshape(n, -1)
    if even_heads:
        bias_full = jnp.zeros((2, nz, n, width // nz), f32)
        bias_full = lax.dynamic_update_slice(
            bias_full, bias_grad.reshape(2, nz, 1, width // nz), (0, 0, p, 0)
        )
    else:
        bias_full = jnp.zeros((2, n, width), f32)
        bias_full = lax.dynamic_update_slice(bias_full, bias_grad.reshape(2, 1, width), (0, p, 0))
    bias_full = bias_full.reshape(2, nz, heads_z * n, head_size // n)
    up_full = jnp.zeros((nz, n, units), f32)
    up_full = lax.dynamic_update_slice(up_full, up_bias_grad.reshape(nz, 1, units), (0, p, 0))
    rows_z = up_bias.shape[0]
    bias_full = bias_full.reshape(2, nz, heads_z, n, head_size // n).transpose(1, 3, 0, 2, 4)
    up_full = up_full.reshape(nz, rows_z, n, up_bias.shape[1]).transpose(0, 2, 1, 3)
    by_slice = jnp.concatenate([bias_full.reshape(nz, n, -1), up_full.reshape(nz, n, -1)], axis=2)

    def for_slice(r):
        return jnp.concatenate(
            [vectors, lax.dynamic_index_in_dim(by_slice, (z + r) % nz, 0, keepdims=False)], axis=1
        )

    table = for_slice(0)
    for r in range(1, nz):
        table = table + turn(for_slice(r), r)
    mine = lax.dynamic_index_in_dim(table, p, 0, keepdims=False)
    for k in range(1, n):
        mine = mine + swap(lax.dynamic_index_in_dim(table, p ^ k, 0, keepdims=False), k)
    vectors = mine[: 6 * shard].reshape(6, shard)
    at = 6 * shard + attention_bias.size
    bias_grad = mine[6 * shard : at].reshape(attention_bias.shape)
    up_bias_grad = mine[at:].reshape(up_bias.shape)
    return (
        output,
        input_grad,
        vectors[0],
        vectors[1],
        in_grad,
        bias_grad,
        out_grad,
        vectors[2],
        vectors[3],
        vectors[4],
        up_grad,
        up_bias_grad,
        down_grad,
        vectors[5],
    )


def solution(mesh):
    return jax.shard_map(
        on_device,
        mesh=mesh,
        in_specs=(
            P("dp", "tensor"),
            P("dp", "tensor"),
            P("dp"),
            P("dp"),
            P(None, "dp", "tensor"),
            P(None, "tensor", "dp"),
            P("tensor", "dp"),
            P("dp"),
            P("dp"),
            P("dp"),
            P("dp", "tensor"),
            P("tensor", "dp"),
            P("tensor", "dp"),
            P("dp"),
            P("dp"),
            P("dp"),
            P("dp"),
            P("dp"),
        ),
        out_specs=(
            P("dp", "tensor"),
            P("dp", "tensor"),
            P("dp"),
            P("dp"),
            P(None, "dp", "tensor"),
            P(None, "tensor", "dp"),
            P("tensor", "dp"),
            P("dp"),
            P("dp"),
            P("dp"),
            P("dp", "tensor"),
            P("tensor", "dp"),
            P("tensor", "dp"),
            P("dp"),
        ),
        check_vma=False,
    )
```

```python
import jax
import jax.numpy as jnp
from jax import lax
from jax.experimental import pallas as pl
from jax.experimental.pallas import tpu as pltpu
from jax.sharding import PartitionSpec as P


H = 32
BLK = 128
MAXLEN = 1024
QB = 512
TILE = 256

norm_eps = 1e-05
masked_score = -1e30
density_scale = 0.3989422804014327
root_half = 0.7071067811865476

f32 = jnp.float32
bf16 = jnp.bfloat16


def normalize(rows):
    mean = jnp.mean(rows, axis=-1, keepdims=True)
    centred = rows - mean
    variance = jnp.mean(centred * centred, axis=-1, keepdims=True)
    scale = lax.rsqrt(variance + norm_eps)
    return (centred * scale, scale)


def norm_back(grad_norm, unit, scale, gain):
    grad_unit = grad_norm * gain
    mean_grad = jnp.mean(grad_unit, axis=-1, keepdims=True)
    mean_dot = jnp.mean(grad_unit * unit, axis=-1, keepdims=True)
    return scale * (grad_unit - mean_grad - unit * mean_dot)


def spread(table):
    return jnp.broadcast_to(table[:, None], (table.shape[0], BLK)).reshape(-1)


def swap(value, k):
    count = lax.axis_size("dp")
    return lax.ppermute(value, "dp", [(i, i ^ k) for i in range(count)])


def turn(value, r):
    count = lax.axis_size("tensor")
    return lax.ppermute(value, "tensor", [(i, (i + r) % count) for i in range(count)])


def after(values, others):
    return lax.optimization_barrier((values, others))[0]


def near_order(bins):
    count = lax.axis_size("dp")
    if count == 8 and bins == 2:
        return [(0, 0), (0, 1), (2, 1), (2, 0), (6, 0), (6, 1), (4, 1), (4, 0)]
    return [(k, b) for k in range(0, count, 2) for b in range(bins)]


def plane_gather(rows, bins):
    if lax.axis_size("dp") == 8 and bins == 2:
        half = rows.shape[0] // 2
        a = swap(rows, 2)
        b = swap(rows, 4)
        c = swap(a[:half], 4)
        d = swap(b[half:], 2)
        pieces = [rows, a[half:], a[:half], c, d, b[half:], b[:half]]
    else:
        pieces = [swap(rows, k) if k else rows for k in range(0, lax.axis_size("dp"), 2)]
    near = jnp.concatenate(pieces, axis=0)
    return near, swap(near, 1)


def sum_pair(near, far, weight, dim):
    other = swap(contract(far, weight, 1, dim).astype(bf16), 1)
    return (contract(near, weight, 1, dim) + other.astype(f32)).astype(bf16)


def sum_first(both, bins):
    count = lax.axis_size("dp")
    step = both.shape[0] * 2 // count
    if count == 8 and bins == 2:
        half = step // 2
        return [swap(both[3 * half : 5 * half], 2), swap(both[5 * half : 7 * half], 4)]
    return [swap(both[j * step : (j + 1) * step], 2 * j) for j in range(1, count // 2)]


def sum_second(both, first, bins):
    if lax.axis_size("dp") == 8 and bins == 2:
        half = both.shape[0] // 8
        a, b = [v.astype(f32) for v in first]
        c = both[7 * half :].astype(f32) + a[half:]
        d = both[2 * half : 3 * half].astype(f32) + b[:half]
        return [c.astype(bf16), d.astype(bf16)]
    return []


def swap_second(values):
    return [swap(value, k) for value, k in zip(values, (4, 2))]


def sum_last(both, first, second, bins):
    count = lax.axis_size("dp")
    step = both.shape[0] * 2 // count
    if count == 8 and bins == 2:
        half = step // 2
        (a, b), (c, d) = [[v.astype(f32) for v in pair] for pair in (first, second)]
        upper = both[:half].astype(f32) + a[:half] + c
        lower = both[half:step].astype(f32) + b[half:] + d
        return jnp.concatenate([upper, lower], axis=0)
    total = both[:step].astype(f32)
    for v in first:
        total = total + v.astype(f32)
    return total


def plane_sum(near, far, weight, dim, bins):
    both = sum_pair(near, far, weight, dim)
    first = sum_first(both, bins)
    second = swap_second(sum_second(both, first, bins))
    return sum_last(both, first, second, bins)


def small_gather(value):
    count = lax.axis_size("dp")
    value = value.reshape(1, -1)
    k = 1
    while k < count:
        value = jnp.concatenate([value, swap(value, k)], axis=0)
        k *= 2
    return jnp.take(value, jnp.arange(count, dtype=jnp.int32) ^ lax.axis_index("dp"), axis=0)


def pick_blocks(rows, wanted):
    count = wanted.shape[0]

    def body(table, source, out):
        for i in range(count):
            begin = pl.multiple_of(table[i] * BLK, BLK)
            out[i * BLK : (i + 1) * BLK, :] = source[pl.ds(begin, BLK), :]

    return pl.pallas_call(
        body,
        out_shape=jax.ShapeDtypeStruct((count * BLK, rows.shape[1]), rows.dtype),
        in_specs=[smem(), vmem()],
        out_specs=vmem(),
        name="pick",
    )(wanted, rows)


def to_bins(pieces):
    count = lax.axis_size("tensor")
    z = lax.axis_index("tensor")
    wide = pieces[0].shape[-1]
    out = jnp.zeros((pieces[0].shape[0], wide * count), pieces[0].dtype)
    for r, piece in enumerate(pieces):
        if r:
            piece = turn(piece, r)
        out = lax.dynamic_update_slice(out, piece, (0, ((z - r) % count) * wide))
    return out


def bin_pieces(rows):
    count = lax.axis_size("tensor")
    z = lax.axis_index("tensor")
    wide = rows.shape[-1] // count
    return [lax.dynamic_slice_in_dim(rows, ((z + r) % count) * wide, wide, 1) for r in range(count)]


def from_bins(pieces):
    return jnp.concatenate([turn(v, r) if r else v for r, v in enumerate(pieces)], axis=0)


def contract(a, b, left, right):
    return lax.dot_general(a, b, (((left,), (right,)), ((), ())), preferred_element_type=f32)


def spread_blocks(bin_block):
    count = lax.axis_size("dp")
    edges = count * count
    levels = count.bit_length() - 1
    assert count == 1 << levels and bin_block.shape == (edges,)

    def body(bin_column, bin_row, color):
        column = lax.broadcasted_iota(jnp.int32, (edges, 1), 0)
        row = lax.broadcasted_iota(jnp.int32, (1, edges), 1)
        here_column, here_row = column, row
        there_column, there_row = bin_column[...], bin_row[...]
        for level in range(levels):
            half = 1 << (levels - level - 1)
            here = jnp.where((here_column ^ 1) == here_row, 1.0, 0.0).astype(bf16)
            there = jnp.where((there_column ^ 1) == there_row, 1.0, 0.0).astype(bf16)
            hop = contract(here, there, 1, 0).astype(bf16)
            least_column, least_row = column.astype(f32), row.astype(f32)
            for _ in range(2 * levels - 1):
                least_column = jnp.minimum(least_column, contract(hop, least_column.astype(bf16), 1, 0))
                least_row = jnp.minimum(least_row, contract(least_row.astype(bf16), hop, 1, 0))
                hop = contract(hop, hop, 1, 0).astype(bf16)
            bit_column = least_column > contract(here, least_column.astype(bf16), 1, 0)
            bit_row = least_row > contract(least_row.astype(bf16), here, 1, 0)

            def refine(key, bit):
                low = key & (2 * half - 1)
                return key - low + jnp.where(bit, half, 0) + (low >> 1)

            here_column, here_row = refine(here_column, bit_column), refine(here_row, bit_row)
            there_column, there_row = refine(there_column, bit_column), refine(there_row, bit_row)
        color[...] = here_row & (count - 1)

    color = pl.pallas_call(
        body, out_shape=jax.ShapeDtypeStruct((1, edges), jnp.int32), name="spread_blocks"
    )(bin_block.reshape(edges, 1), bin_block.reshape(1, edges))
    return color.reshape(count, count)


def attend_kernel(bins, heads, head_size, order, where, slopes, near, far, out_near, out_far, qkv, mixed):
    width = heads * head_size
    for j, b in enumerate(order):
        source, i = (near, j) if j < len(order) // 2 else (far, j - len(order) // 2)
        at = pl.multiple_of(where[j] * BLK, BLK)
        for part in range(3):
            for h in range(heads):
                lo = part * width + h * head_size
                piece = source[i * BLK : (i + 1) * BLK, lo : lo + head_size]
                if part == 0:
                    piece = (piece.astype(f32) * 0.125).astype(bf16)
                qkv[part, b * heads + h, pl.ds(at, BLK), :] = piece
    slots = qkv.shape[2]

    def one_head(h, carry):
        slope = slopes[h % heads]
        for t in range(slots // TILE):
            lo, hi = t * TILE, (t + 1) * TILE
            query = qkv[0, h, lo:hi, :]
            scores = contract(query, qkv[1, h, 0:hi, :], 1, 1)
            column = lax.broadcasted_iota(jnp.int32, (1, hi), 1)
            scores = scores + slope * (column - hi).astype(f32)
            diagonal = scores[:, lo:hi]
            rows = lax.broadcasted_iota(jnp.int32, (TILE, TILE), 0)
            columns = lax.broadcasted_iota(jnp.int32, (TILE, TILE), 1)
            diagonal = jnp.where(columns <= rows, diagonal, masked_score)
            scores = jnp.concatenate([scores[:, :lo], diagonal], axis=1) if t else diagonal
            top = jnp.max(scores, axis=1, keepdims=True)
            weights = jnp.exp(scores - top)
            total = jnp.sum(weights, axis=1, keepdims=True)
            result = contract(weights.astype(bf16), qkv[2, h, 0:hi, :], 1, 0) / total
            mixed[h, lo:hi, :] = result.astype(bf16)
        return carry

    lax.fori_loop(0, bins * heads, one_head, 0)
    for j, b in enumerate(order):
        target, i = (out_near, j) if j < len(order) // 2 else (out_far, j - len(order) // 2)
        at = pl.multiple_of(where[j] * BLK, BLK)
        for h in range(heads):
            target[i * BLK : (i + 1) * BLK, h * head_size : (h + 1) * head_size] = mixed[
                b * heads + h, pl.ds(at, BLK), :
            ]


def attend_back_kernel(
    bins, heads, head_size, order, where, slopes, near, far, grad_near, grad_far, out_near, out_far, qkvg, sums, parts
):
    width = heads * head_size
    for j, b in enumerate(order):
        near_half = j < len(order) // 2
        source, grad, i = (near, grad_near, j) if near_half else (far, grad_far, j - len(order) // 2)
        at = pl.multiple_of(where[j] * BLK, BLK)
        for part in range(4):
            for h in range(heads):
                lo = part * width + h * head_size
                if part < 3:
                    piece = source[i * BLK : (i + 1) * BLK, lo : lo + head_size]
                else:
                    piece = grad[i * BLK : (i + 1) * BLK, h * head_size : (h + 1) * head_size]
                if part == 0:
                    piece = (piece.astype(f32) * 0.125).astype(bf16)
                qkvg[part, b * heads + h, pl.ds(at, BLK), :] = piece
    slots = qkvg.shape[2]

    def one_head(h, carry):
        slope = slopes[h % heads]
        sums[...] = jnp.zeros_like(sums)
        for t in range(slots // TILE):
            lo, hi = t * TILE, (t + 1) * TILE
            query = qkvg[0, h, lo:hi, :]
            grad = qkvg[3, h, lo:hi, :]
            keys = qkvg[1, h, 0:hi, :]
            scores = contract(keys, query, 1, 1)
            key_place = lax.broadcasted_iota(jnp.int32, (hi, 1), 0)
            scores = scores + slope * (key_place - hi).astype(f32)
            diagonal = scores[lo:hi, :]
            rows = lax.broadcasted_iota(jnp.int32, (TILE, TILE), 0)
            columns = lax.broadcasted_iota(jnp.int32, (TILE, TILE), 1)
            diagonal = jnp.where(rows <= columns, diagonal, masked_score)
            scores = jnp.concatenate([scores[:lo, :], diagonal], axis=0) if t else diagonal
            top = jnp.max(scores, axis=0, keepdims=True)
            weights = jnp.exp(scores - top)
            total = jnp.sum(weights, axis=0, keepdims=True)
            probs = weights * (1.0 / total)
            grad_probs = contract(qkvg[2, h, 0:hi, :], grad, 1, 1)
            inner = jnp.sum(probs * grad_probs, axis=0, keepdims=True)
            grad_scores = (probs * (grad_probs - inner)).astype(bf16)
            sums[0, 0:hi, :] += contract(grad_scores, query, 1, 0)
            sums[1, 0:hi, :] += contract(probs.astype(bf16), grad, 1, 0)
            grad_query = contract(grad_scores, keys, 0, 0) * 0.125
            parts[0, h, lo:hi, :] = grad_query.astype(bf16)
        parts[1, h] = sums[0].astype(bf16)
        parts[2, h] = sums[1].astype(bf16)
        return carry

    lax.fori_loop(0, bins * heads, one_head, 0)
    for j, b in enumerate(order):
        target, i = (out_near, j) if j < len(order) // 2 else (out_far, j - len(order) // 2)
        at = pl.multiple_of(where[j] * BLK, BLK)
        for part in range(3):
            for h in range(heads):
                lo = part * width + h * head_size
                target[i * BLK : (i + 1) * BLK, lo : lo + head_size] = parts[
                    part, b * heads + h, pl.ds(at, BLK), :
                ]


def smem():
    return pl.BlockSpec(memory_space=pltpu.SMEM)


def vmem():
    return pl.BlockSpec(memory_space=pltpu.VMEM)


def attend_one(near, far, order, where, slopes, heads, head_size):
    bins = max(order) + 1
    slots = 2 * near.shape[0] // bins
    width = heads * head_size
    half = jax.ShapeDtypeStruct((near.shape[0], width), bf16)

    def body(*refs):
        attend_kernel(bins, heads, head_size, order, *refs)

    return pl.pallas_call(
        body,
        out_shape=(half, half),
        in_specs=[smem(), smem(), vmem(), vmem()],
        out_specs=(vmem(), vmem()),
        scratch_shapes=[
            pltpu.VMEM((3, bins * heads, slots, head_size), bf16),
            pltpu.VMEM((bins * heads, slots, head_size), bf16),
        ],
        cost_estimate=pl.CostEstimate(
            flops=2 * bins * slots * slots * width,
            transcendentals=bins * slots * slots * heads // 2,
            bytes_accessed=8 * bins * slots * width,
        ),
        name="attend",
    )(where, slopes, near, far)


def attend_one_back(near, far, grad_near, grad_far, order, where, slopes, heads, head_size):
    bins = max(order) + 1
    slots = 2 * near.shape[0] // bins
    width = heads * head_size
    half = jax.ShapeDtypeStruct(near.shape, bf16)

    def body(*refs):
        attend_back_kernel(bins, heads, head_size, order, *refs)

    return pl.pallas_call(
        body,
        out_shape=(half, half),
        in_specs=[smem(), smem(), vmem(), vmem(), vmem(), vmem()],
        out_specs=(vmem(), vmem()),
        scratch_shapes=[
            pltpu.VMEM((4, bins * heads, slots, head_size), bf16),
            pltpu.VMEM((2, slots, head_size), f32),
            pltpu.VMEM((3, bins * heads, slots, head_size), bf16),
        ],
        cost_estimate=pl.CostEstimate(
            flops=5 * bins * slots * slots * width,
            transcendentals=bins * slots * slots * heads // 2,
            bytes_accessed=16 * bins * slots * width,
        ),
        name="attend_back",
    )(where, slopes, near, far, grad_near, grad_far)


def block_view(query, keys, values, segment, place, valid, slopes, heads, head_size):
    width = heads * head_size
    keys_pad = jnp.concatenate([jnp.zeros((MAXLEN, width), bf16), keys])
    values_pad = jnp.concatenate([jnp.zeros((MAXLEN, width), bf16), values])
    segment_pad = jnp.concatenate([jnp.full((MAXLEN,), -1, jnp.int32), segment])
    place_pad = jnp.concatenate([jnp.zeros((MAXLEN,), jnp.int32), place])
    valid_pad = jnp.concatenate([jnp.zeros((MAXLEN,), dtype=bool), valid])
    window = QB + MAXLEN

    def block_scores(begin):
        query_block = lax.dynamic_slice_in_dim(query, begin, QB).reshape(QB, heads, head_size)
        key_block = lax.dynamic_slice_in_dim(keys_pad, begin, window).reshape(window, heads, head_size)
        value_block = lax.dynamic_slice_in_dim(values_pad, begin, window).reshape(window, heads, head_size)
        query_segment = lax.dynamic_slice_in_dim(segment, begin, QB)
        query_place = lax.dynamic_slice_in_dim(place, begin, QB)
        key_segment = lax.dynamic_slice_in_dim(segment_pad, begin, window)
        key_place = lax.dynamic_slice_in_dim(place_pad, begin, window)
        key_valid = lax.dynamic_slice_in_dim(valid_pad, begin, window)
        raw = jnp.einsum("qhe,khe->hqk", query_block, key_block, preferred_element_type=f32) * 0.125
        distance = (query_place[:, None] - key_place[None, :]).astype(f32)
        raw = raw - slopes[:, None, None] * distance[None]
        allowed = (
            (query_segment[:, None] == key_segment[None, :])
            & (key_place[None, :] <= query_place[:, None])
            & key_valid[None, :]
        )
        return (jnp.where(allowed[None], raw, masked_score), query_block, key_block, value_block)

    return block_scores, window


def attend_any(query, keys, values, segment, place, valid, slopes, heads, head_size):
    slots, width = query.shape
    block_scores, _ = block_view(query, keys, values, segment, place, valid, slopes, heads, head_size)

    def forward_block(index, attended):
        begin = index * QB
        scores, _, _, value_block = block_scores(begin)
        weights = jax.nn.softmax(scores, axis=-1).astype(bf16)
        mixed = jnp.einsum("hqk,khe->qhe", weights, value_block, preferred_element_type=f32)
        return lax.dynamic_update_slice_in_dim(attended, mixed.reshape(QB, width).astype(bf16), begin, 0)

    return lax.fori_loop(0, slots // QB, forward_block, jnp.zeros((slots, width), bf16))


def attend_any_back(query, keys, values, grad, segment, place, valid, slopes, heads, head_size):
    slots, width = query.shape
    block_scores, window = block_view(query, keys, values, segment, place, valid, slopes, heads, head_size)

    def backward_block(index, carry):
        grad_query, grad_keys, grad_values = carry
        begin = index * QB
        scores, query_block, key_block, value_block = block_scores(begin)
        probs = jax.nn.softmax(scores, axis=-1)
        grad_block = lax.dynamic_slice_in_dim(grad, begin, QB).reshape(QB, heads, head_size)
        grad_probs = jnp.einsum("qhe,khe->hqk", grad_block, value_block, preferred_element_type=f32)
        inner = jnp.sum(probs * grad_probs, axis=-1, keepdims=True)
        grad_scores = (probs * (grad_probs - inner)).astype(bf16)
        query_part = jnp.einsum("hqk,khe->qhe", grad_scores, key_block, preferred_element_type=f32) * 0.125
        key_part = jnp.einsum("hqk,qhe->khe", grad_scores, query_block, preferred_element_type=f32) * 0.125
        value_part = jnp.einsum("hqk,qhe->khe", probs.astype(bf16), grad_block, preferred_element_type=f32)
        grad_query = lax.dynamic_update_slice_in_dim(grad_query, query_part.reshape(QB, width), begin, 0)
        old_keys = lax.dynamic_slice_in_dim(grad_keys, begin, window)
        grad_keys = lax.dynamic_update_slice_in_dim(
            grad_keys, old_keys + key_part.reshape(window, width), begin, 0
        )
        old_values = lax.dynamic_slice_in_dim(grad_values, begin, window)
        grad_values = lax.dynamic_update_slice_in_dim(
            grad_values, old_values + value_part.reshape(window, width), begin, 0
        )
        return (grad_query, grad_keys, grad_values)

    padded_zero = jnp.zeros((MAXLEN + slots, width), f32)
    grad_query, grad_keys, grad_values = lax.fori_loop(
        0, slots // QB, backward_block, (jnp.zeros((slots, width), f32), padded_zero, padded_zero)
    )
    return jnp.concatenate([grad_query, grad_keys[MAXLEN:], grad_values[MAXLEN:]], axis=1).astype(bf16)


def on_device(
    tokens,
    cotangent,
    first_gain,
    first_shift,
    attention_in,
    attention_bias,
    attention_out,
    out_bias,
    second_gain,
    second_shift,
    up_weight,
    up_bias,
    down_weight,
    down_bias,
    source_block,
    target_block,
    block_fill,
    block_start,
):
    n = lax.axis_size("dp")
    nz = lax.axis_size("tensor")
    p = lax.axis_index("dp")
    z = lax.axis_index("tensor")
    bin_slots, _ = tokens.shape
    blocks = bin_slots // BLK
    assert blocks == n and n % nz == 0 and n % 2 == 0
    here = n // nz
    shard = first_gain.shape[0]
    d = shard * n
    head_size = attention_bias.shape[2] * n
    heads_z = attention_bias.shape[1]
    heads = H // n
    width = heads * head_size
    units_z = up_weight.shape[1]
    units = units_z // n
    even_heads = heads_z % n == 0

    small = [first_gain, first_shift, out_bias, second_gain, second_shift, down_bias]
    small = small + [attention_bias.reshape(-1), up_bias.reshape(-1)]
    small = small + [t.astype(bf16) for t in (target_block, block_fill, block_start)]
    packed = small_gather(jnp.concatenate(small))
    at = 6 * shard
    vectors = packed[:, :at].reshape(n, 6, shard).transpose(1, 0, 2).reshape(6, 1, d).astype(f32)
    gain_one, shift_one, out_shift, gain_two, shift_two, down_shift = [vectors[i] for i in range(6)]
    size = attention_bias.size
    bias_z = packed[:, at : at + size].reshape(n, 2, heads_z, head_size // n)
    bias_z = bias_z.transpose(1, 2, 0, 3).reshape(2, heads_z * head_size)
    at = at + size
    size = up_bias.size
    up_z = packed[:, at : at + size].reshape(n, up_bias.shape[0], up_bias.shape[1])
    up_z = up_z.transpose(1, 0, 2).reshape(n, units)
    tables = packed[:, at + size :].reshape(n, 3, blocks).transpose(1, 0, 2).astype(jnp.int32)
    target, fill, start = [tables[i] for i in range(3)]
    if even_heads:
        bias_z = lax.dynamic_slice_in_dim(bias_z, p * (width // nz), width // nz, 1)
        head_ids = jnp.arange(nz, dtype=jnp.int32)[:, None] * heads_z + p * (heads_z // n)
        head_ids = (head_ids + jnp.arange(heads_z // n, dtype=jnp.int32)[None, :]).reshape(-1)
    else:
        head_ids = p * heads + jnp.arange(heads, dtype=jnp.int32)
    up_z = lax.dynamic_index_in_dim(up_z, p, 0, keepdims=False)
    bias_size = bias_z.size
    both_z = jnp.concatenate([bias_z.reshape(-1), up_z])
    every = jnp.zeros((nz, both_z.shape[0]), bf16)
    for r in range(nz):
        piece = turn(both_z, r) if r else both_z
        every = lax.dynamic_update_slice(every, piece[None], ((z - r) % nz, 0))
    mine = every[:, :bias_size].reshape(nz, 2, -1).transpose(1, 0, 2).reshape(2, -1)
    if not even_heads:
        mine = lax.dynamic_slice_in_dim(mine, p * width, width, 1)
    qkv_bias = jnp.concatenate([mine[0], jnp.zeros((width,), bf16), mine[1]]).astype(f32)[None]
    up_shift = every[:, bias_size:].reshape(1, nz * units).astype(f32)
    slopes = jnp.exp2(-8.0 * (head_ids + 1).astype(f32) / H)

    def spread_out(value, split, join):
        return lax.all_to_all(value, "dp", split_axis=split, concat_axis=join, tiled=True)

    def over_bins(value, axis):
        return lax.all_gather(value, "tensor", axis=axis, tiled=True)

    if even_heads:
        in_rows = over_bins(spread_out(attention_in.transpose(0, 2, 1), 1, 2), 1)
    else:
        in_rows = spread_out(over_bins(attention_in, 2).transpose(0, 2, 1), 1, 2)
    in_rows = in_rows.reshape(3 * width, d)
    first_bin = z * here
    ranks = jnp.arange(n, dtype=jnp.int32)
    color = spread_blocks(target.reshape(-1))
    match = color[:, :, None] == ranks[None, None, :]
    held = jnp.sum(jnp.where(match, target[:, :, None], 0), axis=1)
    color = lax.dynamic_index_in_dim(color, p, 0, keepdims=False)
    leave = jnp.sum(jnp.where(color[:, None] == ranks[None, :], ranks[:, None], 0), axis=0)
    held_bin = lax.dynamic_index_in_dim(held // blocks, p, 1, keepdims=False)
    held_by = jnp.sum(jnp.where(held_bin[:, None] == ranks[None, :], ranks[:, None], 0), axis=0)

    ahead = (first_bin + ranks) % n
    at_ahead = held_by[ahead]
    behind = (first_bin + here - 1 - ranks // here * here) % n
    behind = behind - (here - 1) + ranks % here
    place_of = jnp.sum(jnp.where(behind[None, :] == held_bin[:, None], ranks[None, :], 0), axis=1)

    def bring(rows):
        rows = spread_out(pick_blocks(rows, leave), 0, 0)
        return pick_blocks(rows, at_ahead)

    def bring_on(rows):
        return to_bins(jnp.split(rows, nz, axis=0))

    rows_in = bring(tokens)
    cotangent = after(cotangent, rows_in)
    rows_in = bring_on(rows_in)
    if even_heads:
        out_rows = over_bins(spread_out(attention_out, 0, 1), 0)
    else:
        out_rows = spread_out(over_bins(attention_out, 0), 0, 1)
    up_part = over_bins(spread_out(up_weight, 1, 0), 1)
    down_part = over_bins(spread_out(down_weight, 0, 1), 0)
    grad_in = bring(cotangent)

    gathered = near_order(here)
    gathered = gathered + [(k + 1, b) for k, b in gathered]
    order = [b for _, b in gathered]
    of_bin = [held // blocks == first_bin + g for g in range(here)]
    slot_of = jnp.stack([jnp.sum(jnp.where(match, held % blocks, 0), axis=0) for match in of_bin])
    where = slot_of[jnp.array(order), jnp.array([k for k, _ in gathered], jnp.int32) ^ p]
    single = bin_slots == MAXLEN
    offset = jnp.arange(bin_slots, dtype=jnp.int32) % BLK
    block_of = jnp.arange(bin_slots, dtype=jnp.int32) // BLK

    def bin_tables(g):
        bin_start = lax.dynamic_index_in_dim(start, first_bin + g, 0, keepdims=False)
        bin_fill = lax.dynamic_index_in_dim(fill, first_bin + g, 0, keepdims=False)
        segment = spread(bin_start)
        valid = offset < spread(bin_fill)
        place = (block_of - segment) * BLK + offset
        slot = lax.dynamic_index_in_dim(slot_of[g], p, 0, keepdims=False)
        valid_rows = jnp.arange(BLK, dtype=jnp.int32) < lax.dynamic_index_in_dim(bin_fill, slot, 0)
        return segment, place, valid, valid_rows

    sort_key = where + n * jnp.array(order, jnp.int32)
    unsorted = jnp.argsort(sort_key)

    def by_bin(near, far):
        rows = jnp.concatenate([near, far], axis=0).reshape(here * n, BLK, -1)
        return jnp.take(rows, unsorted, axis=0).reshape(here, bin_slots, -1)

    def as_gathered(rows):
        rows = jnp.take(rows.reshape(here * n, BLK, -1), sort_key, axis=0)
        rows = rows.reshape(here * bin_slots, -1)
        return rows[: here * bin_slots // 2], rows[here * bin_slots // 2 :]

    def attend(near, far):
        if single:
            return attend_one(near, far, order, where, slopes, heads, head_size)
        rows = by_bin(near, far)
        mixed = []
        for g in range(here):
            query, keys, values = jnp.split(rows[g], 3, axis=1)
            tables = bin_tables(g)[:3]
            mixed.append(attend_any(query, keys, values, *tables, slopes, heads, head_size))
        return as_gathered(jnp.stack(mixed))

    def attend_back(near, far, grad_near, grad_far):
        if single:
            return attend_one_back(near, far, grad_near, grad_far, order, where, slopes, heads, head_size)
        rows = by_bin(near, far)
        grad = by_bin(grad_near, grad_far)
        grads = []
        for g in range(here):
            query, keys, values = jnp.split(rows[g], 3, axis=1)
            tables = bin_tables(g)[:3]
            grads.append(
                attend_any_back(query, keys, values, grad[g], *tables, slopes, heads, head_size)
            )
        return as_gathered(jnp.stack(grads))

    valid = jnp.concatenate([bin_tables(g)[3] for g in range(here)])[:, None]
    x = rows_in.astype(f32)
    unit_one, scale_one = normalize(x)
    one = plane_gather((unit_one * gain_one + shift_one).astype(bf16), here)
    one = after(one, grad_in)
    grad_in = bring_on(grad_in)
    qkv = [(contract(v, in_rows, 1, 1) + qkv_bias).astype(bf16) for v in one]
    att = attend(*after(qkv, grad_in))
    grad = jnp.where(valid, grad_in.astype(f32), 0.0)
    branch = plane_gather(grad.astype(bf16), here)
    resid = x + plane_sum(*att, out_rows, 0, here) + out_shift
    unit_two, scale_two = normalize(resid)
    norm_two = (unit_two * gain_two + shift_two).astype(bf16)
    two = plane_gather(norm_two, here)
    hidden, slope = [], []
    for v in two:
        before = jnp.dot(v, up_part, preferred_element_type=f32) + up_shift
        share = 0.5 * (1.0 + lax.erf(before * root_half))
        hidden.append((before * share).astype(bf16))
        density = jnp.exp(-0.5 * before * before) * density_scale
        slope.append((share + before * density).astype(bf16))

    def pairs_sum(left, right):
        a = jnp.concatenate(left, axis=0)
        b = jnp.concatenate(right, axis=0)
        return contract(a, b, 0, 0).astype(bf16)

    down_sum = pairs_sum(hidden, branch)
    down_grad = lax.psum_scatter(down_sum, "tensor", scatter_dimension=0, tiled=True)
    grad_before = [
        (contract(v, down_part, 1, 1) * w.astype(f32)).astype(bf16) for v, w in zip(branch, slope)
    ]
    up_sum = pairs_sum(two, grad_before)
    up_grad = lax.psum_scatter(up_sum, "tensor", scatter_dimension=1, tiled=True)
    up_bias_grad = sum(jnp.sum(v.astype(f32), axis=0) for v in grad_before)
    both_two = sum_pair(*grad_before, up_part, 1)
    first_two = sum_first(both_two, here)
    second_two = swap_second(sum_second(both_two, first_two, here))
    grad_two = sum_last(both_two, first_two, second_two, here)
    grad_resid = grad + norm_back(grad_two, unit_two, scale_two, gain_two)
    attn = plane_gather(grad_resid.astype(bf16), here)
    out_grad = pairs_sum(att, attn)
    grad_att = [contract(v, out_rows, 1, 1).astype(bf16) for v in attn]
    both_out = sum_pair(*after(hidden, attn), down_part, 0)
    first_out = sum_first(both_out, here)
    grad_att = after(grad_att, (up_sum, out_grad, both_out))
    grad_qkv = attend_back(*qkv, *grad_att)
    second_out = sum_second(both_out, first_out, here)
    grad_qkv, second_out = lax.optimization_barrier((grad_qkv, second_out))
    second_out = swap_second(second_out)
    both_one = sum_pair(*grad_qkv, in_rows, 0)
    first_one = sum_first(both_one, here)
    result = resid + sum_last(both_out, first_out, second_out, here) + down_shift
    result = jnp.where(valid, result, 0.0).astype(bf16)
    result_pieces = bin_pieces(result)
    output = pick_blocks(from_bins(result_pieces), place_of)
    output = pick_blocks(spread_out(output, 0, 0), color)
    grad_qkv, up_grad, down_grad = after((grad_qkv, up_grad, down_grad), both_one)
    down_grad = spread_out(down_grad, 1, 0).astype(f32)
    up_grad = spread_out(up_grad, 0, 1).astype(f32)
    if even_heads:
        out_grad = lax.psum_scatter(out_grad, "tensor", scatter_dimension=0, tiled=True)
        out_grad = spread_out(after(out_grad, both_one), 1, 0).astype(f32)
    else:
        out_grad = spread_out(out_grad, 1, 0)
        out_grad = lax.psum_scatter(out_grad, "tensor", scatter_dimension=0, tiled=True).astype(f32)
    in_grad = pairs_sum(grad_qkv, one).reshape(3, width, d)
    if even_heads:
        in_grad = in_grad.reshape(3, nz, width // nz, d).transpose(1, 0, 2, 3).reshape(-1, d)
        in_grad = lax.psum_scatter(in_grad, "tensor", scatter_dimension=0, tiled=True)
        in_grad = spread_out(in_grad.reshape(3, width // nz, d), 2, 1)
    else:
        in_grad = spread_out(in_grad, 2, 1)
        in_grad = lax.psum_scatter(in_grad, "tensor", scatter_dimension=1, tiled=True)
    in_grad = in_grad.transpose(0, 2, 1).astype(f32)
    bias_grad = sum(jnp.sum(v.astype(f32), axis=0) for v in grad_qkv)
    bias_grad = jnp.stack([bias_grad[:width], bias_grad[2 * width :]])
    first_one = after(first_one, result_pieces)
    second_one = swap_second(sum_second(both_one, first_one, here))
    grad_one = sum_last(both_one, first_one, second_one, here)
    input_rows = grad_resid + norm_back(grad_one, unit_one, scale_one, gain_one)
    input_grad = pick_blocks(from_bins(bin_pieces(input_rows.astype(bf16))), place_of)
    input_grad = pick_blocks(spread_out(input_grad, 0, 0), color)

    vectors = jnp.stack(
        [
            jnp.sum(grad_one * unit_one, axis=0),
            jnp.sum(grad_one, axis=0),
            jnp.sum(grad_resid, axis=0),
            jnp.sum(grad_two * unit_two, axis=0),
            jnp.sum(grad_two, axis=0),
            jnp.sum(grad, axis=0),
        ]
    ).reshape(6, n, shard).transpose(1, 0, 2).reshape(n, -1)
    if even_heads:
        bias_full = jnp.zeros((2, nz, n, width // nz), f32)
        bias_full = lax.dynamic_update_slice(
            bias_full, bias_grad.reshape(2, nz, 1, width // nz), (0, 0, p, 0)
        )
    else:
        bias_full = jnp.zeros((2, n, width), f32)
        bias_full = lax.dynamic_update_slice(bias_full, bias_grad.reshape(2, 1, width), (0, p, 0))
    bias_full = bias_full.reshape(2, nz, heads_z * n, head_size // n)
    up_full = jnp.zeros((nz, n, units), f32)
    up_full = lax.dynamic_update_slice(up_full, up_bias_grad.reshape(nz, 1, units), (0, p, 0))
    rows_z = up_bias.shape[0]
    bias_full = bias_full.reshape(2, nz, heads_z, n, head_size // n).transpose(1, 3, 0, 2, 4)
    up_full = up_full.reshape(nz, rows_z, n, up_bias.shape[1]).transpose(0, 2, 1, 3)
    by_slice = jnp.concatenate([bias_full.reshape(nz, n, -1), up_full.reshape(nz, n, -1)], axis=2)

    def for_slice(r):
        return jnp.concatenate(
            [vectors, lax.dynamic_index_in_dim(by_slice, (z + r) % nz, 0, keepdims=False)], axis=1
        )

    table = for_slice(0)
    for r in range(1, nz):
        table = table + turn(for_slice(r), r)
    mine = lax.dynamic_index_in_dim(table, p, 0, keepdims=False)
    for k in range(1, n):
        mine = mine + swap(lax.dynamic_index_in_dim(table, p ^ k, 0, keepdims=False), k)
    vectors = mine[: 6 * shard].reshape(6, shard)
    at = 6 * shard + attention_bias.size
    bias_grad = mine[6 * shard : at].reshape(attention_bias.shape)
    up_bias_grad = mine[at:].reshape(up_bias.shape)
    return (
        output,
        input_grad,
        vectors[0],
        vectors[1],
        in_grad,
        bias_grad,
        out_grad,
        vectors[2],
        vectors[3],
        vectors[4],
        up_grad,
        up_bias_grad,
        down_grad,
        vectors[5],
    )


def solution(mesh):
    return jax.shard_map(
        on_device,
        mesh=mesh,
        in_specs=(
            P("dp", "tensor"),
            P("dp", "tensor"),
            P("dp"),
            P("dp"),
            P(None, "dp", "tensor"),
            P(None, "tensor", "dp"),
            P("tensor", "dp"),
            P("dp"),
            P("dp"),
            P("dp"),
            P("dp", "tensor"),
            P("tensor", "dp"),
            P("tensor", "dp"),
            P("dp"),
            P("dp"),
            P("dp"),
            P("dp"),
            P("dp"),
        ),
        out_specs=(
            P("dp", "tensor"),
            P("dp", "tensor"),
            P("dp"),
            P("dp"),
            P(None, "dp", "tensor"),
            P(None, "tensor", "dp"),
            P("tensor", "dp"),
            P("dp"),
            P("dp"),
            P("dp"),
            P("dp", "tensor"),
            P("tensor", "dp"),
            P("tensor", "dp"),
            P("dp"),
        ),
        check_vma=False,
    )
```
